32 devices in a mesh: shard: 2 (over x), ctx: 4 (over z), tp: 4 (over y, core).
Axes of the slice: x: 2, y: 2, z: 4, core: 2. Of those that a mesh axis runs over, the one named last changes fastest.
Arguments:
- hidden_in: bfloat16 [4, 2048, 1152], P('shard', 'ctx'), may hold values from -6 to 6
- cotangent: bfloat16 [4, 2048, 1152], P('shard', 'ctx'), may hold values from -6 to 6
- lengths: int32 [4], P('shard'), may hold values from 512 to 2048, as said below
- positions: int32 [4, 2048], P('shard'), may hold values from 0 to 2047, each once within a row
- w_query: bfloat16 [1152, 1024], P('shard', 'tp'), may hold values from -0.1875 to 0.1875
- w_key: bfloat16 [1152, 256], P('shard'), may hold values from -0.1875 to 0.1875
- w_value: bfloat16 [1152, 256], P('shard'), may hold values from -0.1875 to 0.1875
- w_out: bfloat16 [1024, 1152], P('tp', 'shard'), may hold values from -0.1875 to 0.1875
- w_gate: bfloat16 [1152, 6912], P('shard', 'tp'), may hold values from -0.1875 to 0.1875
- w_up: bfloat16 [1152, 6912], P('shard', 'tp'), may hold values from -0.1875 to 0.1875
- w_down: bfloat16 [6912, 1152], P('tp', 'shard'), may hold values from -0.078125 to 0.078125
- g_input: bfloat16 [1152], P('shard'), may hold values from -0.8984375 to 0.8984375
- g_post_attn: bfloat16 [1152], P('shard'), may hold values from -0.8984375 to 0.8984375
- g_pre_ffn: bfloat16 [1152], P('shard'), may hold values from -0.8984375 to 0.8984375
- g_post_ffn: bfloat16 [1152], P('shard'), may hold values from -0.8984375 to 0.8984375
- q_gain: bfloat16 [256], P('shard'), may hold values from 0 to 1
- k_gain: bfloat16 [256], P('shard'), may hold values from 0 to 1
Outputs:
- out: bfloat16 [4, 2048, 1152], P('shard', 'ctx')
- grad_x: bfloat16 [4, 2048, 1152], P('shard', 'ctx')
- grad_wq: float32 [1152, 1024], P('shard', 'tp')
- grad_wk: float32 [1152, 256], P('shard')
- grad_wv: float32 [1152, 256], P('shard')
- grad_wo: float32 [1024, 1152], P('tp', 'shard')
- grad_w_gate: float32 [1152, 6912], P('shard', 'tp')
- grad_w_up: float32 [1152, 6912], P('shard', 'tp')
- grad_w_down: float32 [6912, 1152], P('tp', 'shard')
- grad_g_input: float32 [1152], P('shard')
- grad_g_post_attn: float32 [1152], P('shard')
- grad_g_pre_ffn: float32 [1152], P('shard')
- grad_g_post_ffn: float32 [1152], P('shard')
- grad_q_gain: float32 [256], P('shard')
- grad_k_gain: float32 [256], P('shard')
The draws below stay inside these ranges and needn't reach their ends.
Inputs may be any that keep to these rules, and one draw needn't show every extreme that they name: `lengths`: each slot holds one sequence; rows at places from its length on are padding. In every draw some slot has length exactly 2048. `positions`: each row of a slot is a permutation of the places 0 to 2047.
All inputs are finite; a program needn't handle non-finite values.
Results may differ from the reference program's by a relative error of at most 0.025.
Values may be sent and summed in bfloat16 or wider, within the bound.
No kernel may reach another device: no remote copies, remote signals or barrier semaphores. Data moves between devices by JAX's collectives and lax.ppermute only.
A program may use at most 256 MiB of HBM per device.

```python
import math
import jax
import jax.numpy as jnp
from jax import lax

D = 1152
HEADS = 4
HEAD_DIM = 256
FF = 6912
SLOT = 2048
SLOTS = 4


def draw_lengths(key, part):
    first_key = jax.random.fold_in(key, 11)
    second_key = jax.random.fold_in(key, 23)
    drawn = jax.random.randint(first_key, (SLOTS,), SLOT // 4, SLOT + 1)
    longest = jax.random.randint(second_key, (), 0, SLOTS)
    return jnp.where(jnp.arange(SLOTS) == longest, SLOT, drawn).astype(jnp.int32)


def block_scale(rng, extent, cuts, low, high):
    def one(axis_at, blocks):
        steps = jax.random.uniform(jax.random.fold_in(jax.random.fold_in(rng, 6), axis_at), (blocks,), jnp.float32, low / len(cuts), high / len(cuts))
        return jnp.repeat(jnp.exp(steps), extent[axis_at] // blocks).reshape((-1,) + (1,) * (len(extent) - axis_at - 1))

    level = one(*cuts[0])
    for cut in cuts[1:]:
        level = level * one(*cut)
    return level


def centred(rng, shape, scale, reach, split=(), kind=jnp.bfloat16):
    array = jax.random.normal(rng, shape, jnp.float32) * scale
    if len(split) > 0:
        array = block_scale(rng, shape, split, -0.22, 0.18) * array
    return jnp.clip(array, min=-reach, max=reach).astype(kind)


def setup_inputs(seed: int = 0) -> dict:
    streams_of = jax.random.split(jax.random.key(seed), 18)
    return {
        "hidden_in": centred(streams_of[0], (SLOTS, SLOT, D), 1.0, 6.0, ((0, 2), (1, 4))),
        "cotangent": centred(streams_of[1], (SLOTS, SLOT, D), 1.0, 6.0, ((0, 2), (1, 4))),
        "lengths": draw_lengths(jax.random.fold_in(streams_of[17], 71), 0),
        "positions": jax.vmap(lambda own: jax.random.permutation(own, SLOT))(jax.random.split(streams_of[3], SLOTS)).reshape((SLOTS, SLOT)).astype(jnp.int32),
        "w_query": centred(streams_of[4], (D, HEADS * HEAD_DIM), D ** -0.5, 0.1875, ((0, 2), (1, 4))),
        "w_key": centred(streams_of[5], (D, HEAD_DIM), D ** -0.5, 0.1875, ((0, 2),)),
        "w_value": centred(streams_of[6], (D, HEAD_DIM), D ** -0.5, 0.1875, ((0, 2),)),
        "w_out": centred(streams_of[7], (HEADS * HEAD_DIM, D), (HEADS * HEAD_DIM) ** -0.5, 0.1875, ((0, 4), (1, 2))),
        "w_gate": centred(streams_of[8], (D, FF), D ** -0.5, 0.1875, ((0, 2), (1, 4))),
        "w_up": centred(streams_of[9], (D, FF), D ** -0.5, 0.1875, ((0, 2), (1, 4))),
        "w_down": centred(streams_of[10], (FF, D), FF ** -0.5, 0.078125, ((0, 4), (1, 2))),
        "g_input": centred(streams_of[11], (D,), 0.3, 0.8984375, ((0, 2),)),
        "g_post_attn": centred(streams_of[12], (D,), 0.3, 0.8984375, ((0, 2),)),
        "g_pre_ffn": centred(streams_of[13], (D,), 0.3, 0.8984375, ((0, 2),)),
        "g_post_ffn": centred(streams_of[14], (D,), 0.3, 0.8984375, ((0, 2),)),
        "q_gain": jnp.clip(1.0 * jax.random.uniform(streams_of[15], (HEAD_DIM,), jnp.float32) ** block_scale(streams_of[15], (HEAD_DIM,), ((0, 2),), -0.2, 0.2), 0.0, 1.0).astype(jnp.bfloat16),
        "k_gain": jnp.clip(1.0 * jax.random.uniform(streams_of[16], (HEAD_DIM,), jnp.float32) ** block_scale(streams_of[16], (HEAD_DIM,), ((0, 2),), -0.2, 0.2), 0.0, 1.0).astype(jnp.bfloat16),
    }


NORM_EPS = 1e-06
PRECISE = lax.Precision.HIGHEST
NEG_LARGE = -1e+30

@jax.custom_vjp
def low(v):
    return lax.optimization_barrier(v.astype(jnp.bfloat16)).astype(jnp.float32)

@jax.custom_vjp
def low_back(v):
    return v

def low_keep(v):
    return (low(v), None)

def low_pass(kept, grad):
    return (grad,)

def back_keep(v):
    return (v, None)

def back_low(kept, grad):
    return (low(grad),)
low.defvjp(low_keep, low_pass)
low_back.defvjp(back_keep, back_low)

def matmul(left, right):
    return jnp.dot(left, right, precision=PRECISE, preferred_element_type=jnp.float32)

def norm_rows(values_in, gain_vec):
    factor = lax.rsqrt(lax.optimization_barrier(jnp.mean(values_in * values_in, axis=-1, keepdims=True)) + NORM_EPS)
    return values_in * factor * (1.0 + gain_vec)

def rotate(values_in, places):
    half_dim = values_in.shape[-1] // 2
    frequency = jnp.exp(jnp.arange(half_dim, dtype=jnp.float32) * (-2.0 * math.log(1000000.0) / values_in.shape[-1]))
    angles = places.astype(jnp.float32)[:, None, None] * frequency
    cosine = jnp.cos(angles)
    sine = jnp.sin(angles)
    first_half = values_in[..., :half_dim]
    second_half = values_in[..., half_dim:]
    return jnp.concatenate([first_half * cosine - second_half * sine, second_half * cosine + first_half * sine], axis=-1)

def attend(queries, keys_all, values_all, places, length):
    block_rows = min(512, SLOT)
    key_live = places < length

    def one_block(pieces):
        query_block, place_block = pieces
        scores = low_back(jnp.einsum('qhd,kd->hqk', query_block, keys_all, precision=PRECISE) * HEAD_DIM ** (-0.5))
        allowed = (places[None, :] <= place_block[:, None]) & key_live[None, :]
        scores = jnp.where(allowed[None], scores, NEG_LARGE)
        row_max = lax.optimization_barrier(jnp.max(scores, axis=-1, keepdims=True))
        expo = jnp.exp(scores - row_max)
        probs = low(expo / lax.optimization_barrier(jnp.sum(expo, axis=-1, keepdims=True)))
        return jnp.einsum('hqk,kd->qhd', probs, values_all, precision=PRECISE)
    blocks = SLOT // block_rows
    mixed = lax.map(jax.checkpoint(one_block), (queries.reshape(blocks, block_rows, HEADS, HEAD_DIM), places.reshape(blocks, block_rows)))
    return mixed.reshape(SLOT, HEADS * HEAD_DIM)

def layer(hidden, weights, places, lengths_in):
    w_query, w_key, w_value, w_out, w_gate, w_up, w_down, g_input, g_post_attn, g_pre_ffn, g_post_ffn, q_gain, k_gain = weights
    group_size = hidden.shape[0]
    flat = hidden.reshape(group_size * SLOT, D)
    flat_places = places.reshape(group_size * SLOT)
    normed = low(norm_rows(flat, g_input))
    queries = low_back(matmul(normed, w_query)).reshape(group_size * SLOT, HEADS, HEAD_DIM)
    keys_raw = low_back(matmul(normed, w_key))
    values_raw = low_back(matmul(normed, w_value))
    query_rot = low(rotate(norm_rows(queries, q_gain), flat_places))
    key_rot = low(rotate(norm_rows(keys_raw[:, None, :], k_gain), flat_places)[:, 0])
    value_low = low(values_raw)
    mixed = jax.vmap(attend)(query_rot.reshape(group_size, SLOT, HEADS, HEAD_DIM), key_rot.reshape(group_size, SLOT, HEAD_DIM), value_low.reshape(group_size, SLOT, HEAD_DIM), places, lengths_in)
    attn_low = low(low_back(mixed.reshape(group_size * SLOT, HEADS * HEAD_DIM)))
    projected = low_back(matmul(attn_low, w_out))
    after_attn = flat + norm_rows(projected, g_post_attn)
    ffn_in = low(norm_rows(after_attn, g_pre_ffn))
    gate_pre = low_back(matmul(ffn_in, w_gate))
    up_pre = low_back(matmul(ffn_in, w_up))
    middle = low(jax.nn.gelu(gate_pre, approximate=True) * up_pre)
    down_out = low_back(matmul(middle, w_down))
    result = after_attn + norm_rows(down_out, g_post_ffn)
    return result.reshape(group_size, SLOT, D)

def reference(hidden_in, cotangent, lengths, positions, w_query, w_key, w_value, w_out, w_gate, w_up, w_down, g_input, g_post_attn, g_pre_ffn, g_post_ffn, q_gain, k_gain):
    weights = tuple((weight_arr.astype(jnp.float32) for weight_arr in (w_query, w_key, w_value, w_out, w_gate, w_up, w_down, g_input, g_post_attn, g_pre_ffn, g_post_ffn, q_gain, k_gain)))
    group_size = math.gcd(SLOTS, max(1, 4096 // SLOT))
    group_count = SLOTS // group_size

    def one_group(totals, pieces):
        hidden, cot_piece, length_piece, place_piece = pieces
        live = (place_piece < length_piece[:, None]).astype(jnp.float32)[:, :, None]
        result, pull = jax.vjp(lambda values_in, params: layer(values_in, params, place_piece, length_piece), hidden.astype(jnp.float32), weights)
        grad_in, grad_params = pull(cot_piece.astype(jnp.float32) * live)
        totals = tuple((total_sum + grad_part for total_sum, grad_part in zip(totals, grad_params)))
        return (totals, (result.astype(jnp.bfloat16), grad_in.astype(jnp.bfloat16)))
    zeros = tuple((jnp.zeros(weight_arr.shape, jnp.float32) for weight_arr in weights))
    totals, (outputs, grads_in) = lax.scan(one_group, zeros, (hidden_in.reshape(group_count, group_size, SLOT, D), cotangent.reshape(group_count, group_size, SLOT, D), lengths.reshape(group_count, group_size), positions.reshape(group_count, group_size, SLOT)))
    return (outputs.reshape(SLOTS, SLOT, D), grads_in.reshape(SLOTS, SLOT, D), totals[0], totals[1], totals[2], totals[3], totals[4], totals[5], totals[6], totals[7], totals[8], totals[9], totals[10], totals[11], totals[12])
```

```python
import math

import jax
import jax.numpy as jnp
from jax import lax
from jax.sharding import PartitionSpec as P

HEAD_DIM = 256
NORM_EPS = 1e-06
NEG_LARGE = -1e30
F32 = jnp.float32
BF16 = jnp.bfloat16

CORE_SWAP = [(0, 1), (1, 0), (2, 3), (3, 2)]
Y_SWAP = [(0, 2), (2, 0), (1, 3), (3, 1)]
Z_PAIRS = [(0, 1), (1, 0), (2, 3), (3, 2)]
SHARD_SWAP = [(0, 1), (1, 0)]


def inv_rms(values_in):
    return lax.rsqrt(jnp.mean(values_in * values_in, axis=-1, keepdims=True) + NORM_EPS)


def norm_rows(values_in, gain_vec):
    return values_in * inv_rms(values_in) * (1.0 + gain_vec)


def norm_back(values_in, gain_vec, upstream):
    c = inv_rms(values_in)
    scaled = upstream * (1.0 + gain_vec)
    d_values = c * scaled - values_in * (c * c * c) * jnp.mean(
        values_in * scaled, axis=-1, keepdims=True
    )
    return d_values, jnp.sum(upstream * values_in * c, axis=0)


def rope(values_in, cosine, sine):
    half = values_in.shape[-1] // 2
    u1, u2 = values_in[..., :half], values_in[..., half:]
    return jnp.concatenate([u1 * cosine - u2 * sine, u2 * cosine + u1 * sine], axis=-1)


def rope_back(values_in, cosine, sine):
    half = values_in.shape[-1] // 2
    d1, d2 = values_in[..., :half], values_in[..., half:]
    return jnp.concatenate([d1 * cosine + d2 * sine, d2 * cosine - d1 * sine], axis=-1)


def mm(left, right):
    return jnp.dot(left, right, preferred_element_type=F32)


def over_rows(left, right):
    return lax.dot_general(left, right, (((0,), (0,)), ((), ())), preferred_element_type=F32)


def against(left, right):
    return lax.dot_general(left, right, (((1,), (1,)), ((), ())), preferred_element_type=F32)


def pick(flag, yes, no):
    return jnp.where(flag, yes, no)


class Links:
    def __init__(self):
        self.n_shard = lax.axis_size("shard")
        self.shard = lax.axis_index("shard")
        self.z = lax.axis_index("ctx")
        self.t = lax.axis_index("tp")
        self.core = lax.rem(self.t, 2)
        self.y = self.t // 2

    def swap_core(self, v):
        return lax.ppermute(v, "tp", CORE_SWAP)

    def swap_y(self, v):
        return lax.ppermute(v, "tp", Y_SWAP)

    def swap_shard(self, v):
        return lax.ppermute(v, "shard", SHARD_SWAP)

    def to_own(self, v):
        v = v.reshape((2, 2) + v.shape[1:])
        v = pick(self.y == 1, v[::-1], v)
        v = pick(self.core == 1, v[:, ::-1], v)
        return jnp.stack([v[0, 0], v[1, 0], v[0, 1], v[1, 1]])

    def from_own(self, v):
        v = jnp.stack([v[0], v[2], v[1], v[3]]).reshape((2, 2) + v.shape[1:])
        v = pick(self.core == 1, v[:, ::-1], v)
        v = pick(self.y == 1, v[::-1], v)
        return v.reshape((4,) + v.shape[2:])

    def reduce_quarters(self, p):
        p = p.astype(BF16)
        r = self.swap_core(p[2:])
        other = (p[1].astype(F32) + r[1].astype(F32)).astype(BF16)
        r2 = self.swap_y(other)
        return p[0].astype(F32) + r[0].astype(F32) + r2.astype(F32)

    def gather_quarters(self, v):
        y = self.swap_y(v)
        c = self.swap_core(v)
        yc = self.swap_core(y)
        return jnp.stack([v, y, c, yc])

    def join(self, own, other, axis):
        first = pick(self.shard == 0, own, other)
        second = pick(self.shard == 0, other, own)
        return jnp.concatenate([first, second], axis)

    def gather_shard(self, v, axis):
        if self.n_shard != 2:
            return lax.all_gather(v, "shard", axis=axis, tiled=True)
        return self.join(v, self.swap_shard(v), axis)

    def gather_shard_shared(self, v, axis):
        if self.n_shard != 2:
            return lax.all_gather(v, "shard", axis=axis, tiled=True)
        half = v.shape[0] // 2
        odd = lax.rem(self.z, 2) == 1
        r = self.swap_shard(pick(odd, v[half:], v[:half]))
        r2 = lax.ppermute(r, "ctx", Z_PAIRS)
        other = jnp.concatenate([pick(odd, r2, r), pick(odd, r, r2)], 0)
        return self.join(v, other, axis)

    def reduce_shard(self, own, other):
        r = self.swap_shard(other.astype(BF16))
        return (own.astype(F32) + r.astype(F32)).astype(BF16)

    def reduce_z(self, v):
        v = lax.optimization_barrier(v.astype(BF16))
        r = lax.ppermute(v, "ctx", [(0, 1), (3, 2)])
        v1 = lax.optimization_barrier((v.astype(F32) + r.astype(F32)).astype(BF16))
        r1 = lax.ppermute(v1, "ctx", [(1, 2), (2, 1)])
        v2 = lax.optimization_barrier((v1.astype(F32) + r1.astype(F32)).astype(BF16))
        r2 = lax.ppermute(v2, "ctx", [(1, 0), (2, 3)])
        inner = (self.z == 1) | (self.z == 2)
        return pick(inner, v2, r2)


def body(
    hidden_in,
    cotangent,
    lengths,
    positions,
    w_query,
    w_key,
    w_value,
    w_out,
    w_gate,
    w_up,
    w_down,
    g_input,
    g_post_attn,
    g_pre_ffn,
    g_post_ffn,
    q_gain,
    k_gain,
):
    ln = Links()
    n_slots, slot_rows, width = hidden_in.shape
    q_rows = slot_rows // 4
    two = ln.n_shard == 2
    wide = width // ln.n_shard
    scale = HEAD_DIM ** (-0.5)

    packed = jnp.concatenate([g_input, g_post_attn, g_pre_ffn, g_post_ffn, q_gain, k_gain])
    gains = ln.gather_shard(packed[None], 0).astype(F32)
    cuts = [0]
    for g in (g_input, g_post_attn, g_pre_ffn, g_post_ffn, q_gain, k_gain):
        cuts.append(cuts[-1] + g.shape[0])
    gain_in, gain_attn, gain_ffn_in, gain_ffn_out, gain_query, gain_key = [
        gains[:, cuts[i] : cuts[i + 1]].reshape(-1) for i in range(6)
    ]
    query_w = ln.gather_shard(w_query, 0)
    if two:
        r = ln.swap_shard(pick(ln.core == 0, w_key, w_value))
        r_c = ln.swap_core(r)
        key_w = ln.join(w_key, pick(ln.core == 0, r, r_c), 0)
        value_w = ln.join(w_value, pick(ln.core == 0, r_c, r), 0)
    else:
        key_w = ln.gather_shard(w_key, 0)
        value_w = ln.gather_shard(w_value, 0)
    out_w = ln.gather_shard(w_out, 1)
    gate_w = ln.gather_shard_shared(w_gate, 0)
    up_w = ln.gather_shard_shared(w_up, 0)
    down_w = ln.gather_shard_shared(w_down, 1)

    frequency = jnp.exp(
        jnp.arange(HEAD_DIM // 2, dtype=F32) * (-2.0 * math.log(1000000.0) / HEAD_DIM)
    )
    own_places = lax.dynamic_slice_in_dim(positions, ln.z * slot_rows, slot_rows, 1)
    slots = range(n_slots)
    rows_at = []
    hid = []
    trig = []
    normed = []
    for s in slots:
        at = ln.to_own(own_places[s].reshape(4, q_rows)).reshape(-1)
        rows_at.append(at)
        angle = at.astype(F32)[:, None] * frequency
        trig.append((jnp.cos(angle), jnp.sin(angle)))
        h = ln.to_own(hidden_in[s].reshape(4, q_rows, width)).reshape(-1, width)
        hid.append(h)
        normed.append(norm_rows(h.astype(F32), gain_in).astype(BF16))

    def core_order(v):
        v = v.reshape((4, q_rows) + v.shape[1:])
        a = jnp.stack([v[0], v[2], v[1], v[3]]).reshape((2, 2, q_rows) + v.shape[2:])
        a = pick(ln.core == 1, a[:, ::-1], a)
        return a.reshape((4 * q_rows,) + v.shape[2:])

    queries, keys_raw, query_rot, key_all, value_all, key_at = [], [], [], [], [], []
    for s in slots:
        cosine, sine = trig[s]
        k_raw = mm(normed[s], key_w)
        v_raw = mm(normed[s], value_w)
        k_rot = rope(norm_rows(k_raw, gain_key), cosine, sine).astype(BF16)
        mine = core_order(pick(ln.core == 0, k_rot, v_raw.astype(BF16)))
        got = [mine]
        for d in (1, 2, 3):
            got.append(lax.ppermute(mine, "ctx", [(i, (i + d) % 4) for i in range(4)]))
        oth = core_order(pick(ln.core == 0, v_raw.astype(BF16), k_rot))
        got_c = [oth] + [ln.swap_core(g) for g in got[1:]]
        a, b = jnp.concatenate(got), jnp.concatenate(got_c)
        key_all.append(pick(ln.core == 0, a, b))
        value_all.append(pick(ln.core == 0, b, a))
        spread = positions[s].reshape(4, 2, slot_rows // 2)
        spread = pick(ln.y == 1, spread[:, ::-1], spread)
        key_at.append(
            jnp.concatenate(
                [
                    lax.dynamic_index_in_dim(spread, lax.rem(ln.z - d + 4, 4), 0, keepdims=False)
                    for d in range(4)
                ]
            ).reshape(-1)
        )
        q_raw = mm(normed[s], query_w)
        queries.append(q_raw)
        keys_raw.append(k_raw)
        query_rot.append(rope(norm_rows(q_raw, gain_query), cosine, sine).astype(BF16))

    def scores_of(s):
        allowed = (key_at[s][None, :] <= rows_at[s][:, None]) & (key_at[s] < lengths[s])[None, :]
        return jnp.where(allowed, against(query_rot[s], key_all[s]) * scale, NEG_LARGE)

    attn_low, log_total, projected = [], [], []
    for s in slots:
        scores = scores_of(s)
        row_max = jnp.max(scores, axis=-1, keepdims=True)
        expo = jnp.exp(scores - row_max)
        totals = jnp.sum(expo, axis=-1, keepdims=True)
        log_total.append(row_max + jnp.log(totals))
        o = (mm(expo.astype(BF16), value_all[s]) / totals).astype(BF16)
        attn_low.append(o)
        projected.append(ln.reduce_quarters(mm(o, out_w).reshape(4, q_rows, width)))

    after, ffn_low = [], []
    for s in slots:
        x1 = hid[s][:q_rows].astype(F32) + norm_rows(projected[s], gain_attn)
        after.append(x1)
        f = norm_rows(x1, gain_ffn_in).astype(BF16)
        ffn_low.append(ln.gather_quarters(f).reshape(-1, width))

    gates, ups, middle, downs = [], [], [], []
    for s in slots:
        gate = mm(ffn_low[s], gate_w)
        up = mm(ffn_low[s], up_w)
        m = (jax.nn.gelu(gate, approximate=True) * up).astype(BF16)
        gates.append(gate.astype(BF16))
        ups.append(up.astype(BF16))
        middle.append(m)
        downs.append(ln.reduce_quarters(mm(m, down_w).reshape(4, q_rows, width)))

    outs, d_down, gys = [], [], []
    sums = {"po": 0.0, "pf": 0.0, "pa": 0.0, "in": 0.0, "q": 0.0, "k": 0.0}
    for s in slots:
        x1 = after[s]
        outs.append((x1 + norm_rows(downs[s], gain_ffn_out)).astype(BF16))
        cot = lax.dynamic_slice_in_dim(cotangent[s], ln.t * q_rows, q_rows, 0)
        live = (rows_at[s][:q_rows] < lengths[s]).astype(F32)[:, None]
        gy = cot.astype(F32) * live
        gys.append(gy)
        dd, dg = norm_back(downs[s], gain_ffn_out, gy)
        sums["po"] += dg
        d_down.append(ln.gather_quarters(dd.astype(BF16)).reshape(-1, width))

    d_gate, d_up, d_ffn_in = [], [], []
    for s in slots:
        d_mid = against(d_down[s], down_w)
        g = gates[s].astype(F32)
        u = ups[s].astype(F32)
        k0 = math.sqrt(2.0 / math.pi)
        th = jnp.tanh(k0 * (g + 0.044715 * g * g * g))
        gel = 0.5 * g * (1.0 + th)
        slope = 0.5 * (1.0 + th) + 0.5 * g * (1.0 - th * th) * k0 * (1.0 + 3 * 0.044715 * g * g)
        dg_ = (d_mid * u * slope).astype(BF16)
        du_ = (d_mid * gel).astype(BF16)
        d_gate.append(dg_)
        d_up.append(du_)
        part = against(dg_, gate_w) + against(du_, up_w)
        d_ffn_in.append(ln.reduce_quarters(part.reshape(4, q_rows, width)))

    f_all = jnp.concatenate(ffn_low)
    m_all = jnp.concatenate(middle)
    dd_all = jnp.concatenate(d_down)
    dg_all = jnp.concatenate(d_gate)
    du_all = jnp.concatenate(d_up)

    def halves(v, axis):
        a, b = jnp.split(v, 2, axis)
        return pick(ln.shard == 0, a, b), pick(ln.shard == 0, b, a)

    if two:
        dd_own, dd_oth = halves(dd_all, 1)
        f_own, f_oth = halves(f_all, 1)
        down_oth = over_rows(m_all, dd_oth).astype(BF16)
        down_own = over_rows(m_all, dd_own)
        sum_down = ln.reduce_shard(down_own, down_oth)
        gate_oth = over_rows(f_oth, dg_all).astype(BF16)
        gate_own = over_rows(f_own, dg_all)
        sum_gate = ln.reduce_shard(gate_own, gate_oth)
        up_oth = over_rows(f_oth, du_all).astype(BF16)
        up_own = over_rows(f_own, du_all)
        sum_up = ln.reduce_shard(up_own, up_oth)
    else:

        def spread_sum(v, axis):
            return lax.psum_scatter(
                v.astype(BF16), "shard", scatter_dimension=axis, tiled=True
            )

        sum_down = spread_sum(over_rows(m_all, dd_all), 1)
        sum_gate = spread_sum(over_rows(f_all, dg_all), 0)
        sum_up = spread_sum(over_rows(f_all, du_all), 0)

    def reduce_z_parts(v, parts):
        step = v.shape[0] // parts
        return jnp.concatenate(
            [ln.reduce_z(v[i * step : (i + 1) * step]) for i in range(parts)]
        ).astype(F32)

    grad_down = reduce_z_parts(sum_down, 2)
    grad_gate = reduce_z_parts(sum_gate, 2)
    grad_up = reduce_z_parts(sum_up, 2)

    d_after, d_proj = [], []
    for s in slots:
        back, dg = norm_back(after[s], gain_ffn_in, d_ffn_in[s])
        sums["pf"] += dg
        da = gys[s] + back
        d_after.append(da)
        dp, dg = norm_back(projected[s], gain_attn, da)
        sums["pa"] += dg
        d_proj.append(ln.gather_quarters(dp.astype(BF16)).reshape(-1, width))

    d_query, d_kv, d_in = [], [], []
    for s in slots:
        d_attn = against(d_proj[s], out_w).astype(BF16)
        probs = jnp.exp(scores_of(s) - log_total[s])
        d_probs = against(d_attn, value_all[s])
        row_dot = jnp.sum(probs * d_probs, axis=-1, keepdims=True)
        d_scores = (probs * (d_probs - row_dot)).astype(BF16)
        d_query_rot = mm(d_scores, key_all[s]) * scale
        d_key_rot = (over_rows(d_scores, query_rot[s]) * scale).astype(BF16)
        d_value = over_rows(probs.astype(BF16), d_attn).astype(BF16)

        half = slot_rows // 2
        keep = pick(ln.core == 0, d_key_rot, d_value)
        give = pick(ln.core == 0, d_value, d_key_rot)
        both = keep.astype(F32) + ln.swap_core(give).astype(F32)
        both = both.reshape(4, 2, half, HEAD_DIM)
        got = ln.swap_y(both[:, 1].astype(BF16))
        chunks = (both[:, 0] + got.astype(F32)).astype(BF16)
        total = chunks[0].astype(F32)
        for d in (1, 2, 3):
            r = lax.ppermute(chunks[d], "ctx", [(i, (i - d) % 4) for i in range(4)])
            total = total + r.astype(F32)
        total = total.reshape(2, q_rows, HEAD_DIM)
        total = pick(ln.core == 1, total[::-1], total).reshape(half, HEAD_DIM)

        def some(v):
            return jnp.concatenate([v[:q_rows], v[2 * q_rows : 3 * q_rows]])

        cosine, sine = trig[s]
        dk, dg = norm_back(
            some(keys_raw[s]), gain_key, rope_back(total, some(cosine), some(sine))
        )
        sums["k"] += pick(ln.core == 0, dg, 0.0)
        dkv = pick(ln.core == 0, dk, total).astype(BF16)
        d_kv.append(dkv)
        dq, dg = norm_back(queries[s], gain_query, rope_back(d_query_rot, cosine, sine))
        sums["q"] += dg
        dq = dq.astype(BF16)
        d_query.append(dq)
        part = against(dq, query_w).reshape(4, q_rows, width)
        extra = against(dkv, pick(ln.core == 0, key_w, value_w)).reshape(2, q_rows, width)
        zero = jnp.zeros_like(extra[0])
        part = part + jnp.stack([extra[0], zero, extra[1], zero])
        d_in.append(ln.reduce_quarters(part))

    def some(v):
        return jnp.concatenate([v[:q_rows], v[2 * q_rows : 3 * q_rows]])

    grad_q = sum(over_rows(normed[s], d_query[s]) for s in slots)
    grad_o = sum(over_rows(d_proj[s], attn_low[s]) for s in slots)
    grad_kv = sum(over_rows(some(normed[s]), d_kv[s]) for s in slots)
    small = jnp.concatenate([grad_o, grad_q, grad_kv], 1)
    if two:
        own, oth = halves(small, 0)
        small = ln.reduce_shard(own, oth)
    else:
        small = spread_sum(small, 0)
    kv = small[:, 2 * HEAD_DIM :]
    kv = (kv.astype(F32) + ln.swap_y(kv).astype(F32)).astype(BF16)
    small = ln.reduce_z(jnp.concatenate([small[:, : 2 * HEAD_DIM], kv], 1))
    grad_wo = small[:, :HEAD_DIM].T.astype(F32)
    grad_wq = small[:, HEAD_DIM : 2 * HEAD_DIM].astype(F32)
    kv = small[:, 2 * HEAD_DIM :]
    kv_c = ln.swap_core(kv)
    grad_wk = pick(ln.core == 0, kv, kv_c).astype(F32)
    grad_wv = pick(ln.core == 0, kv_c, kv).astype(F32)

    grads_x = []
    for s in slots:
        back, dg = norm_back(hid[s][:q_rows].astype(F32), gain_in, d_in[s])
        sums["in"] += dg
        grads_x.append((d_after[s] + back).astype(BF16))

    vec = jnp.concatenate(
        [v.reshape(ln.n_shard, -1) for v in (sums["in"], sums["pa"], sums["pf"], sums["po"], sums["q"], sums["k"])],
        1,
    )
    vec = vec + ln.swap_core(vec)
    vec = vec + ln.swap_y(vec)
    if two:
        vec = vec[ln.shard] + ln.swap_shard(vec[1 - ln.shard])
    else:
        vec = lax.psum_scatter(vec, "shard", scatter_dimension=0, tiled=True)[0]
    vec = vec + lax.ppermute(vec, "ctx", Z_PAIRS)
    vec = vec + lax.ppermute(vec, "ctx", [(0, 2), (2, 0), (1, 3), (3, 1)])
    gain_grads = [vec[cuts[i] : cuts[i + 1]] for i in range(6)]

    def whole_rows(parts):
        full = [ln.from_own(ln.gather_quarters(v)).reshape(slot_rows, width) for v in parts]
        return jnp.stack(full)

    return (
        whole_rows(outs),
        whole_rows(grads_x),
        grad_wq,
        grad_wk,
        grad_wv,
        grad_wo,
        grad_gate,
        grad_up,
        grad_down,
        *gain_grads,
    )


def solution(mesh):
    rows = P("shard", "ctx", None)
    vec = P("shard")
    cols = P("shard", "tp")
    down = P("tp", "shard")
    flat = P("shard", None)
    return jax.shard_map(
        body,
        mesh=mesh,
        in_specs=(rows, rows, vec, flat, cols, flat, flat, down, cols, cols, down)
        + (vec,) * 6,
        out_specs=(rows, rows, cols, flat, flat, down, cols, cols, down) + (vec,) * 6,
        check_vma=False,
    )
```

```python
import math

import jax
import jax.numpy as jnp
from jax import lax
from jax.experimental import pallas as pl
from jax.experimental.pallas import tpu as pltpu
from jax.sharding import PartitionSpec as P

HEAD_DIM = 256
NORM_EPS = 1e-06
NEG_LARGE = -1e30
F32 = jnp.float32
BF16 = jnp.bfloat16

CORE_SWAP = [(0, 1), (1, 0), (2, 3), (3, 2)]
Y_SWAP = [(0, 2), (2, 0), (1, 3), (3, 1)]
Z_PAIRS = [(0, 1), (1, 0), (2, 3), (3, 2)]
SHARD_SWAP = [(0, 1), (1, 0)]


def inv_rms(values_in):
    return lax.rsqrt(jnp.mean(values_in * values_in, axis=-1, keepdims=True) + NORM_EPS)


def norm_rows(values_in, gain_vec):
    return values_in * inv_rms(values_in) * (1.0 + gain_vec)


def norm_back(values_in, gain_vec, upstream):
    c = inv_rms(values_in)
    scaled = upstream * (1.0 + gain_vec)
    d_values = c * scaled - values_in * (c * c * c) * jnp.mean(
        values_in * scaled, axis=-1, keepdims=True
    )
    rows = tuple(range(values_in.ndim - 1))
    return d_values, jnp.sum(upstream * values_in * c, axis=rows)


def rope(values_in, cosine, sine):
    half = values_in.shape[-1] // 2
    u1, u2 = values_in[..., :half], values_in[..., half:]
    return jnp.concatenate([u1 * cosine - u2 * sine, u2 * cosine + u1 * sine], axis=-1)


def rope_back(values_in, cosine, sine):
    half = values_in.shape[-1] // 2
    d1, d2 = values_in[..., :half], values_in[..., half:]
    return jnp.concatenate([d1 * cosine + d2 * sine, d2 * cosine - d1 * sine], axis=-1)


def mm(left, right):
    return jnp.dot(left, right, preferred_element_type=F32)


def over_rows(left, right):
    return lax.dot_general(left, right, (((0,), (0,)), ((), ())), preferred_element_type=F32)


def against(left, right):
    return lax.dot_general(left, right, (((1,), (1,)), ((), ())), preferred_element_type=F32)


def pick(flag, yes, no):
    return jnp.where(flag, yes, no)


def after(first, *values):
    kept = lax.optimization_barrier((first,) + values)[1:]
    return kept[0] if len(kept) == 1 else kept


def cols_swapped(v):
    half = v.shape[-1] // 2
    return jnp.concatenate([v[..., half:], v[..., :half]], axis=-1)


def norm_in_rows(hidden_in, gain_row, places):
    n_slots, slot_rows, width = hidden_in.shape
    q_rows = slot_rows // 4
    blocks = hidden_in.reshape(n_slots * 4, q_rows, width)

    def kernel(places_ref, h_ref, g_ref, normed_ref, own_ref):
        raw = h_ref[0]
        x = raw.astype(F32)
        c = lax.rsqrt(jnp.mean(x * x, axis=-1, keepdims=True) + NORM_EPS)
        first = pl.program_id(0) < n_slots

        def put(v):
            vf = v.astype(F32)
            normed_ref[0] = (vf * c * (1.0 + g_ref[...])).astype(BF16)

            @pl.when(first)
            def _():
                own_ref[0] = v

        @pl.when(places_ref[0] == 0)
        def _():
            put(raw)

        @pl.when(places_ref[0] != 0)
        def _():
            put(cols_swapped(raw))

    return pl.pallas_call(
        kernel,
        grid_spec=pltpu.PrefetchScalarGridSpec(
            num_scalar_prefetch=1,
            grid=(n_slots * 4,),
            in_specs=[
                pl.BlockSpec((1, q_rows, width), lambda i, p: (p[i + 1], 0, 0)),
                pl.BlockSpec((1, width), lambda i, p: (0, 0)),
            ],
            out_specs=[
                pl.BlockSpec((1, q_rows, width), lambda i, p: (i, 0, 0)),
                pl.BlockSpec(
                    (1, q_rows, width), lambda i, p: (jnp.minimum(i, n_slots - 1), 0, 0)
                ),
            ],
        ),
        out_shape=[
            jax.ShapeDtypeStruct((n_slots * 4, q_rows, width), BF16),
            jax.ShapeDtypeStruct((n_slots, q_rows, width), BF16),
        ],
        name="norm_in_rows",
    )(places, blocks, gain_row)


def whole_rows(parts, places, n_slots):
    _, q_rows, width = parts[0].shape

    def kernel(places_ref, *refs):
        out_ref = refs[4]
        for k in range(4):
            at = pl.multiple_of(places_ref[1 + k] * q_rows, q_rows)

            @pl.when(places_ref[0] == 0)
            def _():
                out_ref[0, pl.ds(at, q_rows), :] = refs[k][0]

            @pl.when(places_ref[0] != 0)
            def _():
                out_ref[0, pl.ds(at, q_rows), :] = cols_swapped(refs[k][0])

    return pl.pallas_call(
        kernel,
        grid_spec=pltpu.PrefetchScalarGridSpec(
            num_scalar_prefetch=1,
            grid=(n_slots,),
            in_specs=[pl.BlockSpec((1, q_rows, width), lambda i, p: (i, 0, 0))] * 4,
            out_specs=pl.BlockSpec((1, 4 * q_rows, width), lambda i, p: (i, 0, 0)),
        ),
        out_shape=jax.ShapeDtypeStruct((n_slots, 4 * q_rows, width), BF16),
        name="whole_rows",
    )(places, *parts)


class Links:
    def __init__(self):
        self.n_shard = lax.axis_size("shard")
        self.shard = lax.axis_index("shard")
        self.z = lax.axis_index("ctx")
        self.t = lax.axis_index("tp")
        self.core = lax.rem(self.t, 2)
        self.y = self.t // 2
        c, y = self.core, self.y
        self.quarters = [2 * c + y, 2 * c + 1 - y, 2 * (1 - c) + y, 2 * (1 - c) + 1 - y]

    def swap_core(self, v):
        return lax.ppermute(v, "tp", CORE_SWAP)

    def swap_y(self, v):
        return lax.ppermute(v, "tp", Y_SWAP)

    def swap_shard(self, v):
        return lax.ppermute(v, "shard", SHARD_SWAP)

    def reduce_quarters(self, p):
        q = p.shape[0] // 4
        p = p.astype(BF16)
        r = self.swap_core(p[2 * q :])
        other = (p[q : 2 * q].astype(F32) + r[q:].astype(F32)).astype(BF16)
        r2 = self.swap_y(other)
        return p[:q].astype(F32) + r[:q].astype(F32) + r2.astype(F32)

    def quarters_of(self, v):
        y = self.swap_y(v)
        c = self.swap_core(v)
        yc = self.swap_core(y)
        return [v, y, c, yc]

    def gather_quarters(self, v):
        return jnp.concatenate(self.quarters_of(v))

    def gather_shard(self, v, axis):
        if self.n_shard != 2:
            return lax.all_gather(v, "shard", axis=axis, tiled=True)
        return jnp.concatenate([v, self.swap_shard(v)], axis)

    def reduce_z(self, v):
        r = lax.ppermute(v, "ctx", [(0, 1), (3, 2)])
        v1 = (v.astype(F32) + r.astype(F32)).astype(BF16)
        r1 = lax.ppermute(v1, "ctx", [(1, 2), (2, 1)])
        v2 = (v1.astype(F32) + r1.astype(F32)).astype(BF16)
        r2 = lax.ppermute(v2, "ctx", [(1, 0), (2, 3)])
        inner = (self.z == 1) | (self.z == 2)
        return pick(inner, v2, r2)


def body(
    hidden_in,
    cotangent,
    lengths,
    positions,
    w_query,
    w_key,
    w_value,
    w_out,
    w_gate,
    w_up,
    w_down,
    g_input,
    g_post_attn,
    g_pre_ffn,
    g_post_ffn,
    q_gain,
    k_gain,
):
    ln = Links()
    n, slot_rows, width = hidden_in.shape
    q_rows = slot_rows // 4
    part = n * q_rows
    two = ln.n_shard == 2
    wide = width // ln.n_shard
    scale = HEAD_DIM ** (-0.5)
    slots = range(n)

    swapped = (ln.shard == 1).astype(jnp.int32) if two else jnp.int32(0)
    places = jnp.stack(
        [swapped] + [s * 4 + ln.quarters[k] for k in range(4) for s in slots]
    ).astype(jnp.int32)
    row_places = jnp.stack([swapped] + ln.quarters).astype(jnp.int32)

    gain_in = ln.gather_shard(g_input, 0).astype(F32)
    if two:
        r = ln.swap_shard(pick(ln.core == 0, w_key, w_value))
        r_c = ln.swap_core(r)
        kv_w = jnp.concatenate(
            [
                jnp.concatenate([w_key, w_value], 1),
                jnp.concatenate([pick(ln.core == 0, r, r_c), pick(ln.core == 0, r_c, r)], 1),
            ],
            0,
        )
    else:
        kv_w = ln.gather_shard(jnp.concatenate([w_key, w_value], 1), 0)
    packed = jnp.concatenate([g_post_attn, g_pre_ffn, g_post_ffn, q_gain, k_gain])
    if two:
        gains = jnp.stack([packed, ln.swap_shard(packed)]).astype(F32)
    else:
        gains = lax.all_gather(packed, "shard").astype(F32)
    cuts = [0]
    for g in (g_post_attn, g_pre_ffn, g_post_ffn, q_gain, k_gain):
        cuts.append(cuts[-1] + g.shape[0])
    gain_attn, gain_ffn_in, gain_ffn_out, gain_query, gain_key = [
        gains[:, cuts[i] : cuts[i + 1]].reshape(-1) for i in range(5)
    ]
    if two:
        swap_head = lambda g: pick(swapped == 1, cols_swapped(g), g)
        gain_query, gain_key = swap_head(gain_query), swap_head(gain_key)
    query_w = ln.gather_shard(w_query, 0)
    out_w = ln.gather_shard(w_out, 1)

    frequency = jnp.exp(
        jnp.arange(HEAD_DIM // 2, dtype=F32) * (-2.0 * math.log(1000000.0) / HEAD_DIM)
    )
    key_order = jnp.stack(
        [lax.rem(ln.z - d + 4, 4) * 4 + ln.quarters[k] for k in range(4) for d in range(4)]
    )
    key_at = jnp.take(positions.reshape(n, 16, q_rows), key_order, axis=1)
    rows_at = key_at.reshape(n, 4, 4, q_rows)[:, :, 0].reshape(n, slot_rows)
    key_at = key_at.reshape(n, 16 * q_rows)
    angle = rows_at.astype(F32)[:, :, None] * frequency
    cosine, sine = jnp.cos(angle), jnp.sin(angle)
    cosine_k, sine_k = cosine[:, :q_rows], sine[:, :q_rows]

    normed, hid = norm_in_rows(hidden_in, gain_in[None], places)
    normed = normed.reshape(4 * part, width)
    hid = hid.reshape(part, width)

    kv_raw = mm(normed[:part], kv_w).reshape(n, q_rows, 2 * HEAD_DIM)
    k_raw, v_raw = kv_raw[..., :HEAD_DIM], kv_raw[..., HEAD_DIM:]
    k_rot = rope(norm_rows(k_raw, gain_key), cosine_k, sine_k).astype(BF16)
    kv_own = jnp.concatenate([k_rot, v_raw.astype(BF16)], -1)
    key_all, value_all = [], []
    last = None
    for s in slots:
        mine = kv_own[s]
        got = [mine]
        for d in (1, 2, 3):
            got.append(lax.ppermute(mine, "ctx", [(i, (i + d) % 4) for i in range(4)]))
        last = got[-1]
        zs = jnp.concatenate(got)
        both = jnp.concatenate([zs, ln.swap_y(zs)])
        whole = jnp.concatenate([both, ln.swap_core(both)])
        key_all.append(whole[:, :HEAD_DIM])
        value_all.append(whole[:, HEAD_DIM:])

    if two:
        odd = lax.rem(ln.z, 2) == 1
        ahead = kv_w
        fetched = []
        for w in (w_gate, w_up, w_down):
            half = w.shape[0] // 2
            start = pick(odd, half, 0)
            piece = lax.dynamic_slice_in_dim(w, start, half, 0)
            piece = after(ahead, piece)
            r = ln.swap_shard(piece)
            fetched.append(r)
            ahead = r
        ahead = last
        full = []
        for w, r, axis in zip((w_gate, w_up, w_down), fetched, (0, 0, 1)):
            r2 = lax.ppermute(after(ahead, r), "ctx", Z_PAIRS)
            ahead = r2
            other = jnp.concatenate([pick(odd, r2, r), pick(odd, r, r2)], 0)
            full.append(jnp.concatenate([w, other], axis))
        gate_w, up_w, down_w = full
    else:
        gate_w = ln.gather_shard(w_gate, 0)
        up_w = ln.gather_shard(w_up, 0)
        down_w = ln.gather_shard(w_down, 1)

    def by_slot(v):
        return v.reshape(4, n, q_rows, -1).swapaxes(0, 1).reshape(n, slot_rows, -1)

    def by_quarter(v):
        return v.reshape(n, 4, q_rows, -1).swapaxes(0, 1).reshape(4 * part, -1)

    queries = by_slot(mm(normed, query_w))
    query_rot = rope(norm_rows(queries, gain_query), cosine, sine).astype(BF16)

    def scores_of(s):
        allowed = (key_at[s][None, :] <= rows_at[s][:, None]) & (key_at[s] < lengths[s])[None, :]
        return jnp.where(allowed, against(query_rot[s], key_all[s]) * scale, NEG_LARGE)

    log_total, attn = [], []
    for s in slots:
        scores = scores_of(s)
        row_max = jnp.max(scores, axis=-1, keepdims=True)
        expo = jnp.exp(scores - row_max)
        totals = jnp.sum(expo, axis=-1, keepdims=True)
        log_total.append(row_max + jnp.log(totals))
        attn.append((mm(expo.astype(BF16), value_all[s]) / totals).astype(BF16))
    attn_low = by_quarter(jnp.stack(attn))
    projected = ln.reduce_quarters(mm(attn_low, out_w))

    x1 = hid.astype(F32) + norm_rows(projected, gain_attn)
    ffn_low = ln.gather_quarters(norm_rows(x1, gain_ffn_in).astype(BF16))

    gate = mm(ffn_low, gate_w)
    up = mm(ffn_low, up_w)
    k0 = math.sqrt(2.0 / math.pi)
    th = jnp.tanh(k0 * (gate + 0.044715 * gate * gate * gate))
    gel = 0.5 * gate * (1.0 + th)
    slope = 0.5 * (1.0 + th) + 0.5 * gate * (1.0 - th * th) * k0 * (1.0 + 3 * 0.044715 * gate * gate)
    middle = (gel * up).astype(BF16)
    to_up = gel.astype(BF16)
    to_gate = (up * slope).astype(BF16)
    middle, to_up, to_gate = lax.optimization_barrier((middle, to_up, to_gate))
    down = ln.reduce_quarters(mm(middle, down_w))

    out_own = (x1 + norm_rows(down, gain_ffn_out)).astype(BF16)
    cot = lax.dynamic_slice_in_dim(cotangent, ln.quarters[0] * q_rows, q_rows, 1).reshape(part, width)
    if two:
        cot = pick(swapped == 1, cols_swapped(cot), cot)
    live = (rows_at[:, :q_rows] < lengths[:, None]).astype(F32).reshape(part, 1)
    gy = cot.astype(F32) * live
    dd, dg_ffn_out = norm_back(down, gain_ffn_out, gy)
    d_down = ln.gather_quarters(dd.astype(BF16))

    def to_shards(v):
        return v[:wide], v[wide:]

    def parts_of(v, count):
        step = v.shape[0] // count
        return [v[i * step : (i + 1) * step] for i in range(count)]

    def swap_parts(v, count=2):
        if not two:
            v = lax.psum_scatter(v, "shard", scatter_dimension=0, tiled=True)
            return parts_of(v, count)
        own, oth = to_shards(v)
        return [
            (o.astype(F32) + ln.swap_shard(t).astype(F32)).astype(BF16)
            for o, t in zip(parts_of(own, count), parts_of(oth, count))
        ]

    grad_down_part = over_rows(d_down, middle).astype(BF16)
    sum_down = swap_parts(grad_down_part)
    d_mid = against(d_down, down_w)
    d_gate = (d_mid * to_gate.astype(F32)).astype(BF16)
    d_up = (d_mid * to_up.astype(F32)).astype(BF16)
    d_gate, d_up = after(grad_down_part, d_gate, d_up)
    d_ffn_part = (against(d_gate, gate_w) + against(d_up, up_w)).astype(BF16)
    d_ffn_in = ln.reduce_quarters(d_ffn_part)
    dg_late, du_late = after(d_ffn_part, d_gate, d_up)
    sum_gate = swap_parts(over_rows(ffn_low, dg_late).astype(BF16))
    sum_up = swap_parts(over_rows(ffn_low, du_late).astype(BF16))

    def joined(pieces):
        return jnp.concatenate([ln.reduce_z(v) for v in pieces]).astype(F32)

    grad_down = joined(sum_down).T
    grad_gate = joined(sum_gate)
    grad_up = joined(sum_up)

    back, dg_ffn_in = norm_back(x1, gain_ffn_in, d_ffn_in)
    d_x1 = gy + back
    dp, dg_attn = norm_back(projected, gain_attn, d_x1)
    d_proj = ln.gather_quarters(dp.astype(BF16))

    d_attn = by_slot(against(d_proj, out_w).astype(BF16))
    d_query_rot, d_kv_all = [], []
    for s in slots:
        probs = jnp.exp(scores_of(s) - log_total[s])
        d_probs = against(d_attn[s], value_all[s])
        row_dot = jnp.sum(probs * d_probs, axis=-1, keepdims=True)
        d_scores = (probs * (d_probs - row_dot)).astype(BF16)
        d_query_rot.append(mm(d_scores, key_all[s]) * scale)
        d_key_rot = (over_rows(d_scores, query_rot[s]) * scale).astype(BF16)
        d_value = over_rows(probs.astype(BF16), d_attn[s]).astype(BF16)
        d_kv_all.append(jnp.concatenate([d_key_rot, d_value], 1))
    d_kv_sum = []
    for s in slots:
        v = d_kv_all[s]
        h = v.shape[0] // 2
        v = (v[:h].astype(F32) + ln.swap_core(v[h:]).astype(F32)).astype(BF16)
        h = h // 2
        v = (v[:h].astype(F32) + ln.swap_y(v[h:]).astype(F32)).astype(BF16)
        v = v.reshape(4, q_rows, 2 * HEAD_DIM)
        total = v[0].astype(F32)
        for d in (1, 2, 3):
            r = lax.ppermute(v[d], "ctx", [(i, (i - d) % 4) for i in range(4)])
            total = total + r.astype(F32)
        d_kv_sum.append(total)
    d_kv_sum = jnp.stack(d_kv_sum)
    dk, dg_key = norm_back(
        k_raw, gain_key, rope_back(d_kv_sum[..., :HEAD_DIM], cosine_k, sine_k)
    )
    d_kv = jnp.concatenate([dk, d_kv_sum[..., HEAD_DIM:]], -1).astype(BF16)
    d_kv = d_kv.reshape(part, 2 * HEAD_DIM)

    dq, dg_query = norm_back(queries, gain_query, rope_back(jnp.stack(d_query_rot), cosine, sine))
    d_query = by_quarter(dq.astype(BF16))
    d_in = ln.reduce_quarters(against(d_query, query_w)) + against(d_kv, kv_w)
    back, dg_in = norm_back(hid.astype(F32), gain_in, d_in)
    grad_x_own = (d_x1 + back).astype(BF16)

    grad_kv = over_rows(normed[:part], d_kv).astype(BF16)
    g_k, g_v = grad_kv[:, :HEAD_DIM], grad_kv[:, HEAD_DIM:]
    kv = pick(ln.core == 0, g_k, g_v).astype(F32) + ln.swap_core(
        pick(ln.core == 0, g_v, g_k)
    ).astype(F32)
    kv = kv.astype(BF16)
    kv = (kv.astype(F32) + ln.swap_y(kv).astype(F32)).astype(BF16)
    grad_q = over_rows(normed, d_query).astype(BF16)
    grad_o = over_rows(d_proj, attn_low).astype(BF16)
    small = jnp.concatenate([grad_o, grad_q, kv], 1)
    if two:
        dg_query, dg_key = swap_head(dg_query), swap_head(dg_key)
    vec = jnp.concatenate(
        [v.reshape(ln.n_shard, -1) for v in (dg_in, dg_attn, dg_ffn_in, dg_ffn_out, dg_query, dg_key)],
        1,
    )
    n_vec = vec.shape[1]
    vec = vec + ln.swap_core(vec)
    vec = vec + ln.swap_y(vec)
    cols = small.shape[1]
    tail = jnp.pad(vec, ((0, 0), (0, 16 * cols - n_vec))).reshape(ln.n_shard, 16, cols)
    small = jnp.concatenate([small.reshape(ln.n_shard, wide, cols), tail.astype(BF16)], 1)
    small = small.reshape(ln.n_shard * (wide + 16), cols)
    if two:
        h = wide + 16
        small = (small[:h].astype(F32) + ln.swap_shard(small[h:]).astype(F32)).astype(BF16)
    else:
        small = lax.psum_scatter(small, "shard", scatter_dimension=0, tiled=True)
    small = ln.reduce_z(small)
    vec = small[wide:].reshape(-1)[:n_vec].astype(F32)
    small = small[:wide]
    grad_wo = small[:, :HEAD_DIM].T.astype(F32)
    grad_wq = small[:, HEAD_DIM : 2 * HEAD_DIM].astype(F32)
    kv = small[:, 2 * HEAD_DIM :]
    kv_c = ln.swap_core(kv)
    grad_wk = pick(ln.core == 0, kv, kv_c).astype(F32)
    grad_wv = pick(ln.core == 0, kv_c, kv).astype(F32)

    cuts = [0]
    for g in (g_input, g_post_attn, g_pre_ffn, g_post_ffn, q_gain, k_gain):
        cuts.append(cuts[-1] + g.shape[0])
    gain_grads = [vec[cuts[i] : cuts[i + 1]] for i in range(6)]

    def assembled(v):
        parts = [u.reshape(n, q_rows, width) for u in ln.quarters_of(v)]
        return whole_rows(parts, row_places, n)

    return (
        assembled(out_own),
        assembled(grad_x_own),
        grad_wq,
        grad_wk,
        grad_wv,
        grad_wo,
        grad_gate,
        grad_up,
        grad_down,
        *gain_grads,
    )


def solution(mesh):
    rows = P("shard", "ctx", None)
    vec = P("shard")
    cols = P("shard", "tp")
    down = P("tp", "shard")
    flat = P("shard", None)
    return jax.shard_map(
        body,
        mesh=mesh,
        in_specs=(rows, rows, vec, flat, cols, flat, flat, down, cols, cols, down)
        + (vec,) * 6,
        out_specs=(rows, rows, cols, flat, flat, down, cols, cols, down) + (vec,) * 6,
        check_vma=False,
    )
```

```python
import math

import jax
import jax.numpy as jnp
from jax import lax
from jax.experimental.layout import Layout, with_layout_constraint
from jax.experimental import pallas as pl
from jax.experimental.pallas import tpu as pltpu
from jax.sharding import PartitionSpec as P

HEAD_DIM = 256
NORM_EPS = 1e-06
NEG_LARGE = -1e30
F32 = jnp.float32
BF16 = jnp.bfloat16

CORE_SWAP = [(0, 1), (1, 0), (2, 3), (3, 2)]
Y_SWAP = [(0, 2), (2, 0), (1, 3), (3, 1)]
Z_PAIRS = [(0, 1), (1, 0), (2, 3), (3, 2)]
SHARD_SWAP = [(0, 1), (1, 0)]


def inv_rms(values_in):
    return lax.rsqrt(jnp.mean(values_in * values_in, axis=-1, keepdims=True) + NORM_EPS)


def norm_rows(values_in, gain_vec):
    return values_in * inv_rms(values_in) * (1.0 + gain_vec)


def norm_back(values_in, gain_vec, upstream):
    c = inv_rms(values_in)
    scaled = upstream * (1.0 + gain_vec)
    d_values = c * scaled - values_in * (c * c * c) * jnp.mean(
        values_in * scaled, axis=-1, keepdims=True
    )
    rows = tuple(range(values_in.ndim - 1))
    return d_values, jnp.sum(upstream * values_in * c, axis=rows)


def rope(values_in, cosine, sine):
    half = values_in.shape[-1] // 2
    u1, u2 = values_in[..., :half], values_in[..., half:]
    return jnp.concatenate([u1 * cosine - u2 * sine, u2 * cosine + u1 * sine], axis=-1)


def rope_back(values_in, cosine, sine):
    half = values_in.shape[-1] // 2
    d1, d2 = values_in[..., :half], values_in[..., half:]
    return jnp.concatenate([d1 * cosine + d2 * sine, d2 * cosine - d1 * sine], axis=-1)


def mm(left, right):
    return jnp.dot(left, right, preferred_element_type=F32)


def over_rows(left, right):
    return lax.dot_general(left, right, (((0,), (0,)), ((), ())), preferred_element_type=F32)


def row_major(v):
    return with_layout_constraint(v, Layout(major_to_minor=tuple(range(v.ndim))))


def against(left, right):
    return lax.dot_general(left, right, (((1,), (1,)), ((), ())), preferred_element_type=F32)


def pick(flag, yes, no):
    return jnp.where(flag, yes, no)


def after(first, *values):
    kept = lax.optimization_barrier((first,) + values)[1:]
    return kept[0] if len(kept) == 1 else kept


def cols_swapped(v):
    half = v.shape[-1] // 2
    return jnp.concatenate([v[..., half:], v[..., :half]], axis=-1)


def norm_in_rows(hidden_in, gain_row, places):
    n_slots, slot_rows, width = hidden_in.shape
    q_rows = slot_rows // 4
    blocks = hidden_in.reshape(n_slots * 4, q_rows, width)

    def kernel(places_ref, h_ref, g_ref, normed_ref, own_ref):
        raw = h_ref[0]
        x = raw.astype(F32)
        c = lax.rsqrt(jnp.mean(x * x, axis=-1, keepdims=True) + NORM_EPS)
        first = pl.program_id(0) < n_slots

        def put(v):
            vf = v.astype(F32)
            normed_ref[0] = (vf * c * (1.0 + g_ref[...])).astype(BF16)

            @pl.when(first)
            def _():
                own_ref[0] = v

        @pl.when(places_ref[0] == 0)
        def _():
            put(raw)

        @pl.when(places_ref[0] != 0)
        def _():
            put(cols_swapped(raw))

    return pl.pallas_call(
        kernel,
        grid_spec=pltpu.PrefetchScalarGridSpec(
            num_scalar_prefetch=1,
            grid=(n_slots * 4,),
            in_specs=[
                pl.BlockSpec((1, q_rows, width), lambda i, p: (p[i + 1], 0, 0)),
                pl.BlockSpec((1, width), lambda i, p: (0, 0)),
            ],
            out_specs=[
                pl.BlockSpec((1, q_rows, width), lambda i, p: (i, 0, 0)),
                pl.BlockSpec(
                    (1, q_rows, width), lambda i, p: (jnp.minimum(i, n_slots - 1), 0, 0)
                ),
            ],
        ),
        out_shape=[
            jax.ShapeDtypeStruct((n_slots * 4, q_rows, width), BF16),
            jax.ShapeDtypeStruct((n_slots, q_rows, width), BF16),
        ],
        name="norm_in_rows",
    )(places, blocks, gain_row)


def whole_rows(parts, places, n_slots):
    _, q_rows, width = parts[0].shape

    def kernel(places_ref, *refs):
        out_ref = refs[4]
        for k in range(4):
            at = pl.multiple_of(places_ref[1 + k] * q_rows, q_rows)

            @pl.when(places_ref[0] == 0)
            def _():
                out_ref[0, pl.ds(at, q_rows), :] = refs[k][0]

            @pl.when(places_ref[0] != 0)
            def _():
                out_ref[0, pl.ds(at, q_rows), :] = cols_swapped(refs[k][0])

    return pl.pallas_call(
        kernel,
        grid_spec=pltpu.PrefetchScalarGridSpec(
            num_scalar_prefetch=1,
            grid=(n_slots,),
            in_specs=[pl.BlockSpec((1, q_rows, width), lambda i, p: (i, 0, 0))] * 4,
            out_specs=pl.BlockSpec((1, 4 * q_rows, width), lambda i, p: (i, 0, 0)),
        ),
        out_shape=jax.ShapeDtypeStruct((n_slots, 4 * q_rows, width), BF16),
        name="whole_rows",
    )(places, *parts)


class Links:
    def __init__(self):
        self.n_shard = lax.axis_size("shard")
        self.shard = lax.axis_index("shard")
        self.z = lax.axis_index("ctx")
        self.t = lax.axis_index("tp")
        self.core = lax.rem(self.t, 2)
        self.y = self.t // 2
        c, y = self.core, self.y
        self.quarters = [2 * c + y, 2 * c + 1 - y, 2 * (1 - c) + y, 2 * (1 - c) + 1 - y]

    def swap_core(self, v):
        return lax.ppermute(v, "tp", CORE_SWAP)

    def swap_y(self, v):
        return lax.ppermute(v, "tp", Y_SWAP)

    def swap_shard(self, v):
        return lax.ppermute(v, "shard", SHARD_SWAP)

    def reduce_quarters(self, p):
        q = p.shape[0] // 4
        p = p.astype(BF16)
        r = self.swap_core(p[2 * q :])
        other = (p[q : 2 * q].astype(F32) + r[q:].astype(F32)).astype(BF16)
        r2 = self.swap_y(other)
        return p[:q].astype(F32) + r[:q].astype(F32) + r2.astype(F32)

    def quarters_of(self, v):
        y = self.swap_y(v)
        c = self.swap_core(v)
        yc = self.swap_core(y)
        return [v, y, c, yc]

    def gather_quarters(self, v):
        return jnp.concatenate(self.quarters_of(v))

    def gather_shard(self, v, axis):
        if self.n_shard != 2:
            return lax.all_gather(v, "shard", axis=axis, tiled=True)
        return jnp.concatenate([v, self.swap_shard(v)], axis)


def body(
    hidden_in,
    cotangent,
    lengths,
    positions,
    w_query,
    w_key,
    w_value,
    w_out,
    w_gate,
    w_up,
    w_down,
    g_input,
    g_post_attn,
    g_pre_ffn,
    g_post_ffn,
    q_gain,
    k_gain,
):
    ln = Links()
    n, slot_rows, width = hidden_in.shape
    q_rows = slot_rows // 4
    part = n * q_rows
    two = ln.n_shard == 2
    wide = width // ln.n_shard
    scale = HEAD_DIM ** (-0.5)
    slots = range(n)

    swapped = (ln.shard == 1).astype(jnp.int32) if two else jnp.int32(0)
    places = jnp.stack(
        [swapped] + [s * 4 + ln.quarters[k] for k in range(4) for s in slots]
    ).astype(jnp.int32)
    row_places = jnp.stack([swapped] + ln.quarters).astype(jnp.int32)

    gain_in = ln.gather_shard(g_input, 0).astype(F32)
    if two:
        mix = jnp.concatenate([w_query, pick(ln.core == 0, w_key, w_value)], 1)
        mix = ln.swap_shard(mix)
        query_w = jnp.concatenate([w_query, mix[:, :HEAD_DIM]], 0)
        r = mix[:, HEAD_DIM:]
        r_c = ln.swap_core(r)
        kv_w = jnp.concatenate(
            [
                jnp.concatenate([w_key, w_value], 1),
                jnp.concatenate([pick(ln.core == 0, r, r_c), pick(ln.core == 0, r_c, r)], 1),
            ],
            0,
        )
    else:
        query_w = ln.gather_shard(w_query, 0)
        kv_w = ln.gather_shard(jnp.concatenate([w_key, w_value], 1), 0)
    packed = jnp.concatenate([g_post_attn, g_pre_ffn, g_post_ffn, q_gain, k_gain])
    if two:
        gains = jnp.stack([packed, ln.swap_shard(packed)]).astype(F32)
    else:
        gains = lax.all_gather(packed, "shard").astype(F32)
    cuts = [0]
    for g in (g_post_attn, g_pre_ffn, g_post_ffn, q_gain, k_gain):
        cuts.append(cuts[-1] + g.shape[0])
    gain_attn, gain_ffn_in, gain_ffn_out, gain_query, gain_key = [
        gains[:, cuts[i] : cuts[i + 1]].reshape(-1) for i in range(5)
    ]
    if two:
        swap_head = lambda g: pick(swapped == 1, cols_swapped(g), g)
        gain_query, gain_key = swap_head(gain_query), swap_head(gain_key)
    out_w = ln.gather_shard(w_out, 1)

    odd = lax.rem(ln.z, 2) == 1

    def fetch_x(w):
        half = w.shape[0] // 2
        return ln.swap_shard(lax.dynamic_slice_in_dim(w, pick(odd, half, 0), half, 0))

    def fetch_z(r):
        return lax.ppermute(r, "ctx", Z_PAIRS)

    def complete(w, r, r2, axis):
        other = jnp.concatenate([pick(odd, r2, r), pick(odd, r, r2)], 0)
        return jnp.concatenate([w, other], axis)

    frequency = jnp.exp(
        jnp.arange(HEAD_DIM // 2, dtype=F32) * (-2.0 * math.log(1000000.0) / HEAD_DIM)
    )
    key_order = jnp.stack(
        [lax.rem(ln.z - d + 4, 4) * 4 + ln.quarters[k] for k in range(4) for d in range(4)]
    )
    key_at = jnp.take(positions.reshape(n, 16, q_rows), key_order, axis=1)
    rows_at = key_at.reshape(n, 4, 4, q_rows)[:, :, 0].reshape(n, slot_rows)
    key_at = key_at.reshape(n, 16 * q_rows)
    angle = rows_at.astype(F32)[:, :, None] * frequency
    cosine, sine = jnp.cos(angle), jnp.sin(angle)
    cosine_k, sine_k = cosine[:, :q_rows], sine[:, :q_rows]

    normed, hid = norm_in_rows(hidden_in, gain_in[None], places)
    normed = normed.reshape(4 * part, width)
    hid = hid.reshape(part, width)

    kv_raw = mm(normed[:part], kv_w).reshape(n, q_rows, 2 * HEAD_DIM)
    k_raw, v_raw = kv_raw[..., :HEAD_DIM], kv_raw[..., HEAD_DIM:]
    k_rot = rope(norm_rows(k_raw, gain_key), cosine_k, sine_k).astype(BF16)
    kv_own = jnp.concatenate([k_rot, v_raw.astype(BF16)], -1)
    if two:
        x_gate = fetch_x(w_gate)
        x_gate, kv_own = lax.optimization_barrier((x_gate, kv_own))
    kv_far = [
        lax.ppermute(kv_own, "ctx", [(i, (i + d) % 4) for i in range(4)]) for d in (1, 2, 3)
    ]
    kv_near_y = ln.swap_y(kv_own)
    if two:
        x_up = fetch_x(w_up)
        x_up, kv_far, kv_near_y = lax.optimization_barrier((x_up, kv_far, kv_near_y))
    kv_far = jnp.stack(kv_far, 1)
    kv_far_y = ln.swap_y(kv_far)
    queries = mm(normed, query_w)
    if two:
        z_gate = fetch_z(x_gate)
        x_down = fetch_x(w_down)
        z_gate, x_down, kv_far_y, queries = lax.optimization_barrier(
            (z_gate, x_down, kv_far_y, queries)
        )
    kv_both = jnp.concatenate([kv_own[:, None], kv_far, kv_near_y[:, None], kv_far_y], 1)
    kv_whole = jnp.concatenate([kv_both, ln.swap_core(kv_both)], 1)
    kv_whole = kv_whole.reshape(n, 16 * q_rows, 2 * HEAD_DIM)
    key_all = [kv_whole[s, :, :HEAD_DIM] for s in slots]
    value_all = [kv_whole[s, :, HEAD_DIM:] for s in slots]

    def by_slot(v):
        return v.reshape(4, n, q_rows, -1).swapaxes(0, 1).reshape(n, slot_rows, -1)

    def by_quarter(v):
        return v.reshape(n, 4, q_rows, -1).swapaxes(0, 1).reshape(4 * part, -1)

    queries = by_slot(queries)
    query_rot = rope(norm_rows(queries, gain_query), cosine, sine).astype(BF16)

    def scores_of(s):
        allowed = (key_at[s][None, :] <= rows_at[s][:, None]) & (key_at[s] < lengths[s])[None, :]
        return jnp.where(allowed, against(query_rot[s], key_all[s]) * scale, NEG_LARGE)

    log_total, attn = [], []
    for s in slots:
        scores = scores_of(s)
        row_max = jnp.max(scores, axis=-1, keepdims=True)
        expo = jnp.exp(scores - row_max)
        totals = jnp.sum(expo, axis=-1, keepdims=True)
        log_total.append(row_max + jnp.log(totals))
        attn.append((mm(expo.astype(BF16), value_all[s]) / totals).astype(BF16))
    attn_low = by_quarter(jnp.stack(attn))
    if two:
        z_up = fetch_z(x_up)
        z_up, attn_low = lax.optimization_barrier((z_up, attn_low))
    projected = ln.reduce_quarters(mm(attn_low, out_w))
    if two:
        z_down = fetch_z(x_down)
        z_down, projected = lax.optimization_barrier((z_down, projected))
        gate_w = complete(w_gate, x_gate, z_gate, 0)
        up_w = complete(w_up, x_up, z_up, 0)
        down_w = complete(w_down, x_down, z_down, 1)
    else:
        gate_w = ln.gather_shard(w_gate, 0)
        up_w = ln.gather_shard(w_up, 0)
        down_w = ln.gather_shard(w_down, 1)

    x1 = hid.astype(F32) + norm_rows(projected, gain_attn)
    ffn_low = ln.gather_quarters(norm_rows(x1, gain_ffn_in).astype(BF16))

    gate = mm(ffn_low, gate_w)
    up = mm(ffn_low, up_w)
    k0 = math.sqrt(2.0 / math.pi)
    th = jnp.tanh(k0 * (gate + 0.044715 * gate * gate * gate))
    gel = 0.5 * gate * (1.0 + th)
    slope = 0.5 * (1.0 + th) + 0.5 * gate * (1.0 - th * th) * k0 * (1.0 + 3 * 0.044715 * gate * gate)
    middle = (gel * up).astype(BF16)
    to_up = gel.astype(BF16)
    to_gate = (up * slope).astype(BF16)
    middle, to_up, to_gate = lax.optimization_barrier((middle, to_up, to_gate))
    down = ln.reduce_quarters(mm(middle, down_w))

    out_own = (x1 + norm_rows(down, gain_ffn_out)).astype(BF16)
    cot = lax.dynamic_slice_in_dim(cotangent, ln.quarters[0] * q_rows, q_rows, 1).reshape(part, width)
    if two:
        cot = pick(swapped == 1, cols_swapped(cot), cot)
    live = (rows_at[:, :q_rows] < lengths[:, None]).astype(F32).reshape(part, 1)
    gy = cot.astype(F32) * live
    dd, dg_ffn_out = norm_back(down, gain_ffn_out, gy)
    d_down = ln.gather_quarters(dd.astype(BF16))

    class Piece:
        def __init__(self, own, oth):
            self.v, self.r = own, oth
            self.stage = 0 if two else 1

        def launch(self):
            if self.stage == 0:
                self.r = ln.swap_shard(self.r)
            else:
                if self.stage > 1 or two:
                    self.v = (self.v.astype(F32) + self.r.astype(F32)).astype(BF16)
                pairs = [[(0, 1), (3, 2)], [(1, 2), (2, 1)], [(1, 0), (2, 3)]][self.stage - 1]
                self.r = lax.ppermute(self.v, "ctx", pairs)
            self.stage += 1

        def result(self):
            return pick((ln.z == 1) | (ln.z == 2), self.v, self.r).astype(F32)

    def pieces_of(v, count):
        if not two:
            v = lax.psum_scatter(v, "shard", scatter_dimension=0, tiled=True)
        step = wide // count
        return [
            Piece(
                v[i * step : (i + 1) * step],
                v[wide + i * step : wide + (i + 1) * step] if two else v[:0],
            )
            for i in range(count)
        ]

    def ready(*pieces):
        return [p for p in pieces if p.stage < 4]

    def tick(pieces, *values):
        pieces = ready(*pieces)
        for p in pieces:
            p.launch()
        state, values = lax.optimization_barrier(([(p.v, p.r) for p in pieces], values))
        for p, (v, r) in zip(pieces, state):
            p.v, p.r = v, r
        return values[0] if len(values) == 1 else values

    grad_down_part = row_major(over_rows(d_down, middle).astype(BF16))
    grad_down_part, d_down_late = tick([], grad_down_part, d_down)
    d0, d1 = pieces_of(grad_down_part, 2)
    d_mid = against(d_down_late, down_w)
    d_gate = (d_mid * to_gate.astype(F32)).astype(BF16)
    d_up = (d_mid * to_up.astype(F32)).astype(BF16)
    d_gate, d_up = tick([d0], d_gate, d_up)

    d_part = (against(d_gate, gate_w) + against(d_up, up_w)).astype(BF16)
    d_part_core = ln.swap_core(d_part[2 * part :])
    grad_gate_part = row_major(over_rows(ffn_low, after(d_part, d_gate)).astype(BF16))
    d_part, d_part_core, grad_gate_part, d_up = tick(
        [d0, d1], d_part, d_part_core, grad_gate_part, d_up
    )
    g0, g1 = pieces_of(grad_gate_part, 2)

    near = d_part[part : 2 * part].astype(F32) + d_part_core[part:].astype(F32)
    d_part_y = ln.swap_y(near.astype(BF16))
    grad_up_part = row_major(over_rows(ffn_low, d_up).astype(BF16))
    d_part_y, grad_up_part = tick([d0, d1, g0], d_part_y, grad_up_part)
    u0, u1 = pieces_of(grad_up_part, 2)

    d_ffn_in = (
        d_part[:part].astype(F32) + d_part_core[:part].astype(F32) + d_part_y.astype(F32)
    )
    back, dg_ffn_in = norm_back(x1, gain_ffn_in, d_ffn_in)
    d_x1 = gy + back
    dp, dg_attn = norm_back(projected, gain_attn, d_x1)
    dp = dp.astype(BF16)
    dp_y = ln.swap_y(dp)
    dp, dp_y, d_x1 = tick([d0, d1, g0, g1], dp, dp_y, d_x1)

    dp_both = jnp.concatenate([dp, dp_y])
    d_proj = jnp.concatenate([dp_both, ln.swap_core(dp_both)])
    d_attn = by_slot(against(d_proj, out_w).astype(BF16))

    def attn_back(s):
        probs = jnp.exp(scores_of(s) - log_total[s])
        d_probs = against(d_attn[s], value_all[s])
        row_dot = jnp.sum(probs * d_probs, axis=-1, keepdims=True)
        d_scores = (probs * (d_probs - row_dot)).astype(BF16)
        d_query_rot = mm(d_scores, key_all[s]) * scale
        d_key_rot = (over_rows(d_scores, query_rot[s]) * scale).astype(BF16)
        d_value = over_rows(probs.astype(BF16), d_attn[s]).astype(BF16)
        return d_query_rot, jnp.concatenate([d_key_rot, d_value], 1)

    def near_core(v):
        h = v.shape[0] // 2
        return (v[:h].astype(F32) + ln.swap_core(v[h:]).astype(F32)).astype(BF16)

    def near_y(v):
        h = v.shape[0] // 2
        return (v[:h].astype(F32) + ln.swap_y(v[h:]).astype(F32)).astype(BF16)

    def to_owner(v):
        v = v.reshape(4, q_rows, 2 * HEAD_DIM)
        total = v[0].astype(F32)
        for d in (1, 2, 3):
            r = lax.ppermute(v[d], "ctx", [(i, (i - d) % 4) for i in range(4)])
            total = total + r.astype(F32)
        return total

    d_query_rot, d_kv = [], []
    for s in slots:
        dq_s, dkv_s = attn_back(s)
        d_query_rot.append(dq_s)
        d_kv = d_kv + [dkv_s]
        group = ready(d0, d1, g0, g1, u0, u1)[:4]
        d_attn, d_query_rot, d_kv, d_proj = tick(group, d_attn, d_query_rot, d_kv, d_proj)
        if s == 0:
            d_kv = [near_core(d_kv[0])]
    d_kv = d_kv[:1] + [near_core(v) for v in d_kv[1:]]

    d_kv = [near_y(v) for v in d_kv]
    dq, dg_query = norm_back(queries, gain_query, rope_back(jnp.stack(d_query_rot), cosine, sine))
    d_query = by_quarter(dq.astype(BF16))
    group = ready(d0, d1, g0, g1, u0, u1)[:4]
    d_kv, d_query, d_proj = tick(group, d_kv, d_query, d_proj)

    grad_oq = jnp.concatenate(
        [over_rows(d_proj, attn_low).astype(BF16), over_rows(normed, d_query).astype(BF16)], 1
    )
    (oq,) = pieces_of(grad_oq, 1)
    d_kv_sum = [to_owner(v) for v in d_kv]
    group = ready(d0, d1, g0, g1, u0, u1, oq)[:4]
    d_kv_sum, d_query, grad_oq = tick(group, d_kv_sum, d_query, grad_oq)

    d_kv_sum = jnp.stack(d_kv_sum)
    dk, dg_key = norm_back(
        k_raw, gain_key, rope_back(d_kv_sum[..., :HEAD_DIM], cosine_k, sine_k)
    )
    d_kv = jnp.concatenate([dk, d_kv_sum[..., HEAD_DIM:]], -1).astype(BF16)
    d_kv = d_kv.reshape(part, 2 * HEAD_DIM)
    grad_kv = over_rows(normed[:part], d_kv).astype(BF16)
    g_k, g_v = grad_kv[:, :HEAD_DIM], grad_kv[:, HEAD_DIM:]
    kv = pick(ln.core == 0, g_k, g_v).astype(F32) + ln.swap_core(
        pick(ln.core == 0, g_v, g_k)
    ).astype(F32)
    kv = kv.astype(BF16)
    kv_y = ln.swap_y(kv)
    d_in = ln.reduce_quarters(against(d_query, query_w)) + against(d_kv, kv_w)
    group = ready(d0, d1, g0, g1, u0, u1, oq)[:3]
    kv, kv_y, d_in = tick(group, kv, kv_y, d_in)

    back, dg_in = norm_back(hid.astype(F32), gain_in, d_in)
    grad_x_own = (d_x1 + back).astype(BF16)
    kv = (kv.astype(F32) + kv_y.astype(F32)).astype(BF16)
    if two:
        dg_query, dg_key = swap_head(dg_query), swap_head(dg_key)
    vec = jnp.concatenate(
        [v.reshape(ln.n_shard, -1) for v in (dg_in, dg_attn, dg_ffn_in, dg_ffn_out, dg_query, dg_key)],
        1,
    )
    n_vec = vec.shape[1]
    vec = vec + ln.swap_core(vec)
    vec = vec + ln.swap_y(vec)
    tail = jnp.pad(vec, ((0, 0), (0, 16 * HEAD_DIM - n_vec))).reshape(ln.n_shard, 16, HEAD_DIM)
    tail = jnp.concatenate([kv.reshape(ln.n_shard, wide, HEAD_DIM), tail.astype(BF16)], 1)
    if two:
        last = Piece(tail[0], tail[1])
    else:
        tail = tail.reshape(ln.n_shard * (wide + 16), HEAD_DIM)
        last = Piece(lax.psum_scatter(tail, "shard", scatter_dimension=0, tiled=True), tail[:0])
    while ready(oq, last, d0, d1, g0, g1, u0, u1):
        group = ready(d0, d1, g0, g1, u0, u1, oq, last)[:4]
        tick(group, jnp.zeros((), F32))

    grad_down = jnp.concatenate([d0.result(), d1.result()]).T
    grad_gate = jnp.concatenate([g0.result(), g1.result()])
    grad_up = jnp.concatenate([u0.result(), u1.result()])
    small = oq.result()
    grad_wo = small[:, :HEAD_DIM].T
    grad_wq = small[:, HEAD_DIM:]
    small = last.result()
    vec = small[wide:].reshape(-1)[:n_vec]
    kv = small[:wide].astype(BF16)
    kv_c = ln.swap_core(kv)
    grad_wk = pick(ln.core == 0, kv, kv_c).astype(F32)
    grad_wv = pick(ln.core == 0, kv_c, kv).astype(F32)

    cuts = [0]
    for g in (g_input, g_post_attn, g_pre_ffn, g_post_ffn, q_gain, k_gain):
        cuts.append(cuts[-1] + g.shape[0])
    gain_grads = [vec[cuts[i] : cuts[i + 1]] for i in range(6)]

    def assembled(v):
        parts = [u.reshape(n, q_rows, width) for u in ln.quarters_of(v)]
        return whole_rows(parts, row_places, n)

    return (
        assembled(after(grad_x_own, out_own)),
        assembled(grad_x_own),
        grad_wq,
        grad_wk,
        grad_wv,
        grad_wo,
        grad_gate,
        grad_up,
        grad_down,
        *gain_grads,
    )


def solution(mesh):
    rows = P("shard", "ctx", None)
    vec = P("shard")
    cols = P("shard", "tp")
    down = P("tp", "shard")
    flat = P("shard", None)
    return jax.shard_map(
        body,
        mesh=mesh,
        in_specs=(rows, rows, vec, flat, cols, flat, flat, down, cols, cols, down)
        + (vec,) * 6,
        out_specs=(rows, rows, cols, flat, flat, down, cols, cols, down) + (vec,) * 6,
        check_vma=False,
    )
```

```python
import math

import jax
import jax.numpy as jnp
from jax import lax
from jax.experimental.layout import Layout, with_layout_constraint
from jax.experimental import pallas as pl
from jax.experimental.pallas import tpu as pltpu
from jax.sharding import PartitionSpec as P

HEAD_DIM = 256
NORM_EPS = 1e-06
NEG_LARGE = -1e30
F32 = jnp.float32
BF16 = jnp.bfloat16

CORE_SWAP = [(0, 1), (1, 0), (2, 3), (3, 2)]
Y_SWAP = [(0, 2), (2, 0), (1, 3), (3, 1)]
Z_PAIRS = [(0, 1), (1, 0), (2, 3), (3, 2)]
SHARD_SWAP = [(0, 1), (1, 0)]


def inv_rms(values_in):
    return lax.rsqrt(jnp.mean(values_in * values_in, axis=-1, keepdims=True) + NORM_EPS)


def norm_rows(values_in, gain_vec):
    return values_in * inv_rms(values_in) * (1.0 + gain_vec)


def norm_back(values_in, gain_vec, upstream):
    c = inv_rms(values_in)
    scaled = upstream * (1.0 + gain_vec)
    d_values = c * scaled - values_in * (c * c * c) * jnp.mean(
        values_in * scaled, axis=-1, keepdims=True
    )
    rows = tuple(range(values_in.ndim - 1))
    return d_values, jnp.sum(upstream * values_in * c, axis=rows)


def rope(values_in, cosine, sine):
    half = values_in.shape[-1] // 2
    u1, u2 = values_in[..., :half], values_in[..., half:]
    return jnp.concatenate([u1 * cosine - u2 * sine, u2 * cosine + u1 * sine], axis=-1)


def rope_back(values_in, cosine, sine):
    half = values_in.shape[-1] // 2
    d1, d2 = values_in[..., :half], values_in[..., half:]
    return jnp.concatenate([d1 * cosine + d2 * sine, d2 * cosine - d1 * sine], axis=-1)


def mm(left, right):
    return jnp.dot(left, right, preferred_element_type=F32)


def over_rows(left, right):
    return lax.dot_general(left, right, (((0,), (0,)), ((), ())), preferred_element_type=F32)


def row_major(v):
    return with_layout_constraint(v, Layout(major_to_minor=tuple(range(v.ndim))))


def against(left, right):
    return lax.dot_general(left, right, (((1,), (1,)), ((), ())), preferred_element_type=F32)


def pick(flag, yes, no):
    return jnp.where(flag, yes, no)


def after(first, *values):
    kept = lax.optimization_barrier((first,) + values)[1:]
    return kept[0] if len(kept) == 1 else kept


def cols_swapped(v):
    half = v.shape[-1] // 2
    return jnp.concatenate([v[..., half:], v[..., :half]], axis=-1)


def norm_in_rows(hidden_in, gain_row, places):
    n_slots, slot_rows, width = hidden_in.shape
    q_rows = slot_rows // 4
    blocks = hidden_in.reshape(n_slots * 4, q_rows, width)

    def kernel(places_ref, h_ref, g_ref, normed_ref, own_ref):
        raw = h_ref[0]
        x = raw.astype(F32)
        c = lax.rsqrt(jnp.mean(x * x, axis=-1, keepdims=True) + NORM_EPS)
        first = pl.program_id(0) < n_slots

        def put(v):
            vf = v.astype(F32)
            normed_ref[0] = (vf * c * (1.0 + g_ref[...])).astype(BF16)

            @pl.when(first)
            def _():
                own_ref[0] = v

        @pl.when(places_ref[0] == 0)
        def _():
            put(raw)

        @pl.when(places_ref[0] != 0)
        def _():
            put(cols_swapped(raw))

    return pl.pallas_call(
        kernel,
        grid_spec=pltpu.PrefetchScalarGridSpec(
            num_scalar_prefetch=1,
            grid=(n_slots * 4,),
            in_specs=[
                pl.BlockSpec((1, q_rows, width), lambda i, p: (p[i + 1], 0, 0)),
                pl.BlockSpec((1, width), lambda i, p: (0, 0)),
            ],
            out_specs=[
                pl.BlockSpec((1, q_rows, width), lambda i, p: (i, 0, 0)),
                pl.BlockSpec(
                    (1, q_rows, width), lambda i, p: (jnp.minimum(i, n_slots - 1), 0, 0)
                ),
            ],
        ),
        out_shape=[
            jax.ShapeDtypeStruct((n_slots * 4, q_rows, width), BF16),
            jax.ShapeDtypeStruct((n_slots, q_rows, width), BF16),
        ],
        name="norm_in_rows",
    )(places, blocks, gain_row)


def whole_rows(parts, places, n_slots):
    _, q_rows, width = parts[0].shape

    def kernel(places_ref, *refs):
        out_ref = refs[4]
        for k in range(4):
            at = pl.multiple_of(places_ref[1 + k] * q_rows, q_rows)

            @pl.when(places_ref[0] == 0)
            def _():
                out_ref[0, pl.ds(at, q_rows), :] = refs[k][0]

            @pl.when(places_ref[0] != 0)
            def _():
                out_ref[0, pl.ds(at, q_rows), :] = cols_swapped(refs[k][0])

    return pl.pallas_call(
        kernel,
        grid_spec=pltpu.PrefetchScalarGridSpec(
            num_scalar_prefetch=1,
            grid=(n_slots,),
            in_specs=[pl.BlockSpec((1, q_rows, width), lambda i, p: (i, 0, 0))] * 4,
            out_specs=pl.BlockSpec((1, 4 * q_rows, width), lambda i, p: (i, 0, 0)),
        ),
        out_shape=jax.ShapeDtypeStruct((n_slots, 4 * q_rows, width), BF16),
        name="whole_rows",
    )(places, *parts)


class Links:
    def __init__(self):
        self.n_shard = lax.axis_size("shard")
        self.shard = lax.axis_index("shard")
        self.z = lax.axis_index("ctx")
        self.t = lax.axis_index("tp")
        self.core = lax.rem(self.t, 2)
        self.y = self.t // 2
        c, y = self.core, self.y
        self.quarters = [2 * c + y, 2 * c + 1 - y, 2 * (1 - c) + y, 2 * (1 - c) + 1 - y]

    def swap_core(self, v):
        return lax.ppermute(v, "tp", CORE_SWAP)

    def swap_y(self, v):
        return lax.ppermute(v, "tp", Y_SWAP)

    def swap_shard(self, v):
        return lax.ppermute(v, "shard", SHARD_SWAP)

    def reduce_quarters(self, p):
        q = p.shape[0] // 4
        p = p.astype(BF16)
        r = self.swap_core(p[2 * q :])
        other = (p[q : 2 * q].astype(F32) + r[q:].astype(F32)).astype(BF16)
        r2 = self.swap_y(other)
        return p[:q].astype(F32) + r[:q].astype(F32) + r2.astype(F32)

    def quarters_of(self, v):
        y = self.swap_y(v)
        c = self.swap_core(v)
        yc = self.swap_core(y)
        return [v, y, c, yc]

    def gather_quarters(self, v):
        return jnp.concatenate(self.quarters_of(v))

    def gather_shard(self, v, axis):
        if self.n_shard != 2:
            return lax.all_gather(v, "shard", axis=axis, tiled=True)
        return jnp.concatenate([v, self.swap_shard(v)], axis)


def body(
    hidden_in,
    cotangent,
    lengths,
    positions,
    w_query,
    w_key,
    w_value,
    w_out,
    w_gate,
    w_up,
    w_down,
    g_input,
    g_post_attn,
    g_pre_ffn,
    g_post_ffn,
    q_gain,
    k_gain,
):
    ln = Links()
    n, slot_rows, width = hidden_in.shape
    q_rows = slot_rows // 4
    part = n * q_rows
    two = ln.n_shard == 2
    wide = width // ln.n_shard
    scale = HEAD_DIM ** (-0.5)
    slots = range(n)

    swapped = (ln.shard == 1).astype(jnp.int32) if two else jnp.int32(0)
    places = jnp.stack(
        [swapped] + [s * 4 + ln.quarters[k] for k in range(4) for s in slots]
    ).astype(jnp.int32)
    row_places = jnp.stack([swapped] + ln.quarters).astype(jnp.int32)

    gain_in = ln.gather_shard(g_input, 0).astype(F32)
    if two:
        mix = jnp.concatenate([w_query, pick(ln.core == 0, w_key, w_value)], 1)
        mix, gain_in = lax.optimization_barrier((ln.swap_shard(mix), gain_in))
        query_w = jnp.concatenate([w_query, mix[:, :HEAD_DIM]], 0)
        r = mix[:, HEAD_DIM:]
        r_c = ln.swap_core(r)
        kv_w = jnp.concatenate(
            [
                jnp.concatenate([w_key, w_value], 1),
                jnp.concatenate([pick(ln.core == 0, r, r_c), pick(ln.core == 0, r_c, r)], 1),
            ],
            0,
        )
    else:
        query_w = ln.gather_shard(w_query, 0)
        kv_w = ln.gather_shard(jnp.concatenate([w_key, w_value], 1), 0)
    packed = jnp.concatenate([g_post_attn, g_pre_ffn, g_post_ffn, q_gain, k_gain])
    if two:
        gains = jnp.stack([packed, ln.swap_shard(packed)]).astype(F32)
    else:
        gains = lax.all_gather(packed, "shard").astype(F32)
    cuts = [0]
    for g in (g_post_attn, g_pre_ffn, g_post_ffn, q_gain, k_gain):
        cuts.append(cuts[-1] + g.shape[0])
    gain_attn, gain_ffn_in, gain_ffn_out, gain_query, gain_key = [
        gains[:, cuts[i] : cuts[i + 1]].reshape(-1) for i in range(5)
    ]
    if two:
        swap_head = lambda g: pick(swapped == 1, cols_swapped(g), g)
        gain_query, gain_key = swap_head(gain_query), swap_head(gain_key)
    out_w = ln.gather_shard(w_out, 1)

    odd = lax.rem(ln.z, 2) == 1

    def fetch_x(w):
        half = w.shape[0] // 2
        w = after(mix, w)
        return ln.swap_shard(lax.dynamic_slice_in_dim(w, pick(odd, half, 0), half, 0))

    def fetch_z(r):
        return lax.ppermute(r, "ctx", Z_PAIRS)

    def complete(w, r, r2, axis):
        other = jnp.concatenate([pick(odd, r2, r), pick(odd, r, r2)], 0)
        return jnp.concatenate([w, other], axis)

    frequency = jnp.exp(
        jnp.arange(HEAD_DIM // 2, dtype=F32) * (-2.0 * math.log(1000000.0) / HEAD_DIM)
    )
    key_order = jnp.stack(
        [lax.rem(ln.z - d + 4, 4) * 4 + ln.quarters[k] for k in range(4) for d in range(4)]
    )
    key_at = jnp.take(positions.reshape(n, 16, q_rows), key_order, axis=1)
    rows_at = key_at.reshape(n, 4, 4, q_rows)[:, :, 0].reshape(n, slot_rows)
    key_at = key_at.reshape(n, 16 * q_rows)
    angle = rows_at.astype(F32)[:, :, None] * frequency
    cosine, sine = jnp.cos(angle), jnp.sin(angle)
    cosine_k, sine_k = cosine[:, :q_rows], sine[:, :q_rows]

    normed, hid = norm_in_rows(hidden_in, gain_in[None], places)
    normed = normed.reshape(4 * part, width)
    hid = hid.reshape(part, width)

    kv_raw = mm(normed[:part], kv_w).reshape(n, q_rows, 2 * HEAD_DIM)
    k_raw, v_raw = kv_raw[..., :HEAD_DIM], kv_raw[..., HEAD_DIM:]
    k_rot = rope(norm_rows(k_raw, gain_key), cosine_k, sine_k).astype(BF16)
    kv_own = jnp.concatenate([k_rot, v_raw.astype(BF16)], -1)
    kv_far = [
        lax.ppermute(kv_own, "ctx", [(i, (i + d) % 4) for i in range(4)]) for d in (1, 2, 3)
    ]
    kv_near_y = ln.swap_y(kv_own)
    queries = mm(normed, query_w)
    if two:
        x_gate = fetch_x(w_gate)
        x_gate, kv_far, kv_near_y, queries = lax.optimization_barrier(
            (x_gate, kv_far, kv_near_y, queries)
        )
    kv_far = jnp.stack(kv_far, 1)
    kv_far_y = ln.swap_y(kv_far)
    kv_both = jnp.concatenate([kv_own[:, None], kv_far, kv_near_y[:, None], kv_far_y], 1)
    kv_whole = jnp.concatenate([kv_both, ln.swap_core(kv_both)], 1)
    kv_whole = kv_whole.reshape(n, 16 * q_rows, 2 * HEAD_DIM)
    key_all = [kv_whole[s, :, :HEAD_DIM] for s in slots]
    value_all = [kv_whole[s, :, HEAD_DIM:] for s in slots]

    def by_slot(v):
        return v.reshape(4, n, q_rows, -1).swapaxes(0, 1).reshape(n, slot_rows, -1)

    def by_quarter(v):
        return v.reshape(n, 4, q_rows, -1).swapaxes(0, 1).reshape(4 * part, -1)

    queries = by_slot(queries)
    query_rot = rope(norm_rows(queries, gain_query), cosine, sine).astype(BF16)

    def scores_of(s):
        allowed = (key_at[s][None, :] <= rows_at[s][:, None]) & (key_at[s] < lengths[s])[None, :]
        return jnp.where(allowed, against(query_rot[s], key_all[s]) * scale, NEG_LARGE)

    log_total, attn = [], []
    for s in slots:
        scores = scores_of(s)
        row_max = jnp.max(scores, axis=-1, keepdims=True)
        expo = jnp.exp(scores - row_max)
        totals = jnp.sum(expo, axis=-1, keepdims=True)
        log_total.append(row_max + jnp.log(totals))
        attn.append((mm(expo.astype(BF16), value_all[s]) / totals).astype(BF16))
    attn_low = by_quarter(jnp.stack(attn))
    if two:
        z_gate = fetch_z(x_gate)
        x_up = fetch_x(w_up)
        z_gate, x_up, attn_low = lax.optimization_barrier((z_gate, x_up, attn_low))
    projected = ln.reduce_quarters(mm(attn_low, out_w))
    if two:
        z_up = fetch_z(x_up)
        x_down = fetch_x(w_down)
        z_up, x_down, projected = lax.optimization_barrier((z_up, x_down, projected))
        gate_w = complete(w_gate, x_gate, z_gate, 0)
        up_w = complete(w_up, x_up, z_up, 0)
    else:
        gate_w = ln.gather_shard(w_gate, 0)
        up_w = ln.gather_shard(w_up, 0)
        down_w = ln.gather_shard(w_down, 1)

    x1 = hid.astype(F32) + norm_rows(projected, gain_attn)
    ffn_low = ln.gather_quarters(norm_rows(x1, gain_ffn_in).astype(BF16))

    gate = mm(ffn_low, gate_w)
    up = mm(ffn_low, up_w)
    k0 = math.sqrt(2.0 / math.pi)
    th = jnp.tanh(k0 * (gate + 0.044715 * gate * gate * gate))
    gel = 0.5 * gate * (1.0 + th)
    slope = 0.5 * (1.0 + th) + 0.5 * gate * (1.0 - th * th) * k0 * (1.0 + 3 * 0.044715 * gate * gate)
    middle = (gel * up).astype(BF16)
    to_up = gel.astype(BF16)
    to_gate = (up * slope).astype(BF16)
    if two:
        z_down = fetch_z(x_down)
        middle, to_up, to_gate, z_down = lax.optimization_barrier((middle, to_up, to_gate, z_down))
        down_w = complete(w_down, x_down, z_down, 1)
    down = ln.reduce_quarters(mm(middle, down_w))

    out_own = (x1 + norm_rows(down, gain_ffn_out)).astype(BF16)
    cot = lax.dynamic_slice_in_dim(cotangent, ln.quarters[0] * q_rows, q_rows, 1).reshape(part, width)
    if two:
        cot = pick(swapped == 1, cols_swapped(cot), cot)
    live = (rows_at[:, :q_rows] < lengths[:, None]).astype(F32).reshape(part, 1)
    gy = cot.astype(F32) * live
    dd, dg_ffn_out = norm_back(down, gain_ffn_out, gy)
    d_down = ln.gather_quarters(dd.astype(BF16))

    inner = (ln.z == 1) | (ln.z == 2)

    alive = []

    def added(u, v):
        return (u.astype(F32) + v.astype(F32)).astype(BF16)

    class Piece:
        def __init__(self, own, oth, stage):
            self.v, self.r, self.stage = own, oth, stage
            alive.append(self)

        def over_shard(self):
            self.v, self.r = added(self.v, ln.swap_shard(self.r)), self.r[:0]

        def middle_hop(self):
            self.r = lax.ppermute(self.v, "ctx", [(1, 2), (2, 1)])

    def outer_hops(inward, outward):
        if outward is None:
            inward.v = added(inward.v, lax.ppermute(inward.v, "ctx", [(0, 1), (3, 2)]))
            return
        total = added(outward.v, outward.r)
        if inward is None:
            r = lax.ppermute(total, "ctx", [(1, 0), (2, 3)])
        else:
            r = lax.ppermute(pick(inner, total, inward.v), "ctx", Z_PAIRS)
            inward.v = added(inward.v, r)
        outward.v, outward.r = pick(inner, total, r), outward.r[:0]

    def pieces_of(v, count):
        v = row_major(v)
        if not two:
            v = lax.psum_scatter(v, "shard", scatter_dimension=0, tiled=True)
        step = wide // count
        return [
            Piece(
                v[i * step : (i + 1) * step],
                v[wide + i * step : wide + (i + 1) * step] if two else v[:0],
                0 if two else 1,
            )
            for i in range(count)
        ]

    def ready(*pieces):
        return [p for p in pieces if p.stage < 4]

    def tick(pieces, *values):
        pieces = ready(*pieces)
        inward = [p for p in pieces if p.stage == 1]
        outward = [p for p in pieces if p.stage == 3]
        for p in inward:
            same = [q for q in outward if q.v.shape == p.v.shape][:1]
            outer_hops(p, same[0] if same else None)
            outward = [q for q in outward if q not in same]
        for q in outward:
            outer_hops(None, q)
        for p in pieces:
            if p.stage == 0:
                p.over_shard()
            elif p.stage == 2:
                p.middle_hop()
            p.stage += 1
        state, values = lax.optimization_barrier(([(p.v, p.r) for p in alive], values))
        for p, (v, r) in zip(alive, state):
            p.v, p.r = v, r
        alive[:] = ready(*alive)
        return values[0] if len(values) == 1 else values

    grad_down_part = row_major(over_rows(d_down, middle).astype(BF16))
    grad_down_part, d_down_late = tick([], grad_down_part, d_down)
    d0, d1 = pieces_of(grad_down_part, 2)

    d_mid = against(d_down_late, down_w)
    d_gate = (d_mid * to_gate.astype(F32)).astype(BF16)
    d_up = (d_mid * to_up.astype(F32)).astype(BF16)
    d_part = against(d_gate, gate_w)
    d_gate, d_up, d_part = tick([d0], d_gate, d_up, d_part)
    d_part = (d_part + against(d_up, up_w)).astype(BF16)
    d_part_core = ln.swap_core(d_part[2 * part :])
    grad_gate_part = row_major(over_rows(ffn_low, after(d_part, d_gate)).astype(BF16))
    d_up, d_part, d_part_core, grad_gate_part = tick(
        [d0, d1], d_up, d_part, d_part_core, grad_gate_part
    )
    g0, g1 = pieces_of(grad_gate_part, 2)

    d_part_y = ln.swap_y(added(d_part[part : 2 * part], d_part_core[part:]))
    grad_up_part = row_major(over_rows(ffn_low, d_up).astype(BF16))
    d_part_y, grad_up_part = lax.optimization_barrier((d_part_y, grad_up_part))
    d_ffn_in = (
        d_part[:part].astype(F32) + d_part_core[:part].astype(F32) + d_part_y.astype(F32)
    )
    back, dg_ffn_in = norm_back(x1, gain_ffn_in, d_ffn_in)
    d_x1 = gy + back
    dp, dg_attn = norm_back(projected, gain_attn, d_x1)
    dp = dp.astype(BF16)
    dp_y = ln.swap_y(dp)
    grad_up_part, dp, d_x1 = tick([d0, d1, g0], grad_up_part, dp, d_x1)
    u0, u1 = pieces_of(grad_up_part, 2)

    dp_both = jnp.concatenate([dp, dp_y])
    d_proj = jnp.concatenate([dp_both, ln.swap_core(dp_both)])
    out_y = ln.swap_y(after(dp_y, out_own))
    d_attn = by_slot(against(d_proj, out_w).astype(BF16))

    def attn_back(s):
        probs = jnp.exp(scores_of(s) - log_total[s])
        d_probs = against(d_attn[s], value_all[s])
        row_dot = jnp.sum(probs * d_probs, axis=-1, keepdims=True)
        d_scores = (probs * (d_probs - row_dot)).astype(BF16)
        d_query_rot = mm(d_scores, key_all[s]) * scale
        d_key_rot = (over_rows(d_scores, query_rot[s]) * scale).astype(BF16)
        d_value = over_rows(probs.astype(BF16), d_attn[s]).astype(BF16)
        return d_query_rot, jnp.concatenate([d_key_rot, d_value], 1)

    d_query_rot, d_kv = [], []
    for s in slots:
        dq_s, dkv_s = attn_back(s)
        h = dkv_s.shape[0] // 2
        d_query_rot.append(dq_s)
        d_kv.append(added(dkv_s[:h], ln.swap_core(dkv_s[h:])))
    d_kv = jnp.stack(d_kv)
    d_query_rot, d_kv, d_proj, out_y, out_own = tick(
        [d0, d1, g0, g1], d_query_rot, d_kv, d_proj, out_y, out_own
    )

    h = d_kv.shape[1] // 2
    d_kv = added(d_kv[:, :h], ln.swap_y(d_kv[:, h:])).reshape(n, 4, q_rows, 2 * HEAD_DIM)
    out_c = ln.swap_core(out_own)
    dq, dg_query = norm_back(queries, gain_query, rope_back(jnp.stack(d_query_rot), cosine, sine))
    d_query = by_quarter(dq.astype(BF16))
    d_kv, d_query, out_c = tick([d1, g0, g1, u0], d_kv, d_query, out_c)

    far = [
        lax.ppermute(d_kv[:, d], "ctx", [(i, (i - d) % 4) for i in range(4)]) for d in (1, 2, 3)
    ]
    d_in_part = against(d_query, query_w).astype(BF16)
    d_in_core = ln.swap_core(d_in_part[2 * part :])
    grad_oq = jnp.concatenate(
        [over_rows(d_proj, attn_low).astype(BF16), over_rows(normed, d_query).astype(BF16)], 1
    )
    far, d_kv, d_in_part, d_in_core, grad_oq = tick(
        [u1] if two else [], far, d_kv, d_in_part, d_in_core, grad_oq
    )
    (oq,) = pieces_of(grad_oq, 1)

    d_in_near = added(d_in_part[part : 2 * part], d_in_core[part:])
    d_kv_sum = (
        d_kv[:, 0].astype(F32) + far[0].astype(F32) + far[1].astype(F32) + far[2].astype(F32)
    )
    d_in_y = ln.swap_y(after(d_kv_sum, d_in_near))
    dk, dg_key = norm_back(
        k_raw, gain_key, rope_back(d_kv_sum[..., :HEAD_DIM], cosine_k, sine_k)
    )
    d_kv = jnp.concatenate([dk, d_kv_sum[..., HEAD_DIM:]], -1).astype(BF16)
    d_kv = d_kv.reshape(part, 2 * HEAD_DIM)
    grad_kv = over_rows(normed[:part], d_kv).astype(BF16)
    g_k, g_v = grad_kv[:, :HEAD_DIM], grad_kv[:, HEAD_DIM:]
    kv = pick(ln.core == 0, g_k, g_v).astype(F32) + ln.swap_core(
        pick(ln.core == 0, g_v, g_k)
    ).astype(F32)
    d_in_own = against(d_kv, kv_w)
    dg_in = (
        jnp.sum(d_in_part.astype(F32) * normed.astype(F32), axis=0)
        + jnp.sum(d_in_own * normed[:part].astype(F32), axis=0)
    ) / (1.0 + gain_in)
    if two:
        dg_query, dg_key = swap_head(dg_query), swap_head(dg_key)
    vec = jnp.concatenate(
        [v.reshape(ln.n_shard, -1) for v in (dg_in, dg_attn, dg_ffn_in, dg_ffn_out, dg_query, dg_key)],
        1,
    )
    n_vec = vec.shape[1]
    vec = vec + ln.swap_core(vec)
    tail = jnp.pad(vec, ((0, 0), (0, 16 * HEAD_DIM - n_vec))).reshape(ln.n_shard, 16, HEAD_DIM)
    tail = jnp.concatenate([kv.reshape(ln.n_shard, wide, HEAD_DIM), tail], 1).astype(BF16)
    if two:
        tail = added(tail[0], ln.swap_shard(tail[1]))
    else:
        tail = tail.reshape(ln.n_shard * (wide + 16), HEAD_DIM)
        tail = lax.psum_scatter(tail, "shard", scatter_dimension=0, tiled=True)
    tail, d_in_y, d_in_own = tick([g0, g1, u0, oq], tail, d_in_y, d_in_own)

    tail = added(tail, ln.swap_y(tail))
    d_in = (
        d_in_part[:part].astype(F32)
        + d_in_core[:part].astype(F32)
        + d_in_y.astype(F32)
        + d_in_own
    )
    grad_x_own = (d_x1 + norm_back(hid.astype(F32), gain_in, d_in)[0]).astype(BF16)
    grad_down = jnp.concatenate([d0.v, d1.v]).T.astype(F32)
    tail, grad_x_own, grad_down = tick([g1, u0, u1], tail, grad_x_own, grad_down)
    last = Piece(tail, tail[:0], 1)

    gx_y = ln.swap_y(grad_x_own)
    gx_y = tick([last, u0, u1, oq], gx_y)
    gx_c, gx_yc, out_yc = ln.swap_core(grad_x_own), ln.swap_core(gx_y), ln.swap_core(out_y)
    grad_gate = jnp.concatenate([g0.v, g1.v]).astype(F32)
    gx_c, gx_yc, out_yc, grad_gate = tick([last, oq, u1], gx_c, gx_yc, out_yc, grad_gate)
    while ready(last, oq, d0, d1, g0, g1, u0, u1):
        tick([last, oq, d0, d1, g0, g1, u0, u1])

    grad_up = jnp.concatenate([u0.v, u1.v]).astype(F32)
    small = oq.v.astype(F32)
    grad_wo = small[:, :HEAD_DIM].T
    grad_wq = small[:, HEAD_DIM:]
    small = last.v
    vec = small[wide:].reshape(-1)[:n_vec].astype(F32)
    kv = small[:wide]
    kv_c = ln.swap_core(kv)
    grad_wk = pick(ln.core == 0, kv, kv_c).astype(F32)
    grad_wv = pick(ln.core == 0, kv_c, kv).astype(F32)

    cuts = [0]
    for g in (g_input, g_post_attn, g_pre_ffn, g_post_ffn, q_gain, k_gain):
        cuts.append(cuts[-1] + g.shape[0])
    gain_grads = [vec[cuts[i] : cuts[i + 1]] for i in range(6)]

    def assembled(parts):
        return whole_rows([u.reshape(n, q_rows, width) for u in parts], row_places, n)

    return (
        assembled([out_own, out_y, out_c, out_yc]),
        assembled([grad_x_own, gx_y, gx_c, gx_yc]),
        grad_wq,
        grad_wk,
        grad_wv,
        grad_wo,
        grad_gate,
        grad_up,
        grad_down,
        *gain_grads,
    )


def solution(mesh):
    rows = P("shard", "ctx", None)
    vec = P("shard")
    cols = P("shard", "tp")
    down = P("tp", "shard")
    flat = P("shard", None)
    return jax.shard_map(
        body,
        mesh=mesh,
        in_specs=(rows, rows, vec, flat, cols, flat, flat, down, cols, cols, down)
        + (vec,) * 6,
        out_specs=(rows, rows, cols, flat, flat, down, cols, cols, down) + (vec,) * 6,
        check_vma=False,
    )
```

```python
import math

import jax
import jax.numpy as jnp
from jax import lax
from jax.experimental.layout import Layout, with_layout_constraint
from jax.experimental import pallas as pl
from jax.experimental.pallas import tpu as pltpu
from jax.sharding import PartitionSpec as P

HEAD_DIM = 256
NORM_EPS = 1e-06
NEG_LARGE = -1e30
F32 = jnp.float32
BF16 = jnp.bfloat16

CORE_SWAP = [(0, 1), (1, 0), (2, 3), (3, 2)]
Y_SWAP = [(0, 2), (2, 0), (1, 3), (3, 1)]
Z_PAIRS = [(0, 1), (1, 0), (2, 3), (3, 2)]
SHARD_SWAP = [(0, 1), (1, 0)]


def inv_rms(values_in):
    return lax.rsqrt(jnp.mean(values_in * values_in, axis=-1, keepdims=True) + NORM_EPS)


def norm_rows(values_in, gain_vec):
    return values_in * inv_rms(values_in) * (1.0 + gain_vec)


def norm_back(values_in, gain_vec, upstream):
    c = inv_rms(values_in)
    scaled = upstream * (1.0 + gain_vec)
    d_values = c * scaled - values_in * (c * c * c) * jnp.mean(
        values_in * scaled, axis=-1, keepdims=True
    )
    return d_values


def gain_back(values_in, upstream):
    rows = tuple(range(values_in.ndim - 1))
    return jnp.sum(upstream * values_in * inv_rms(values_in), axis=rows)


def rope(values_in, cosine, sine):
    half = values_in.shape[-1] // 2
    u1, u2 = values_in[..., :half], values_in[..., half:]
    return jnp.concatenate([u1 * cosine - u2 * sine, u2 * cosine + u1 * sine], axis=-1)


def rope_back(values_in, cosine, sine):
    half = values_in.shape[-1] // 2
    d1, d2 = values_in[..., :half], values_in[..., half:]
    return jnp.concatenate([d1 * cosine + d2 * sine, d2 * cosine - d1 * sine], axis=-1)


def mm(left, right):
    return jnp.dot(left, right, preferred_element_type=F32)


def over_rows(left, right):
    return lax.dot_general(left, right, (((0,), (0,)), ((), ())), preferred_element_type=F32)


def row_major(v):
    return with_layout_constraint(v, Layout(major_to_minor=tuple(range(v.ndim))))


def against(left, right):
    return lax.dot_general(left, right, (((1,), (1,)), ((), ())), preferred_element_type=F32)


def pick(flag, yes, no):
    return jnp.where(flag, yes, no)


def after(first, *values):
    kept = lax.optimization_barrier((first,) + values)[1:]
    return kept[0] if len(kept) == 1 else kept


def cols_swapped(v):
    half = v.shape[-1] // 2
    return jnp.concatenate([v[..., half:], v[..., :half]], axis=-1)


def norm_in_rows(hidden_in, gain_row, places):
    n_slots, slot_rows, width = hidden_in.shape
    q_rows = slot_rows // 4
    blocks = hidden_in.reshape(n_slots * 4, q_rows, width)

    def kernel(places_ref, h_ref, g_ref, normed_ref, own_ref):
        raw = h_ref[0]
        x = raw.astype(F32)
        c = lax.rsqrt(jnp.mean(x * x, axis=-1, keepdims=True) + NORM_EPS)
        first = pl.program_id(0) < n_slots

        def put(v):
            vf = v.astype(F32)
            normed_ref[0] = (vf * c * (1.0 + g_ref[...])).astype(BF16)

            @pl.when(first)
            def _():
                own_ref[0] = v

        @pl.when(places_ref[0] == 0)
        def _():
            put(raw)

        @pl.when(places_ref[0] != 0)
        def _():
            put(cols_swapped(raw))

    return pl.pallas_call(
        kernel,
        grid_spec=pltpu.PrefetchScalarGridSpec(
            num_scalar_prefetch=1,
            grid=(n_slots * 4,),
            in_specs=[
                pl.BlockSpec((1, q_rows, width), lambda i, p: (p[i + 1], 0, 0)),
                pl.BlockSpec((1, width), lambda i, p: (0, 0)),
            ],
            out_specs=[
                pl.BlockSpec((1, q_rows, width), lambda i, p: (i, 0, 0)),
                pl.BlockSpec(
                    (1, q_rows, width), lambda i, p: (jnp.minimum(i, n_slots - 1), 0, 0)
                ),
            ],
        ),
        out_shape=[
            jax.ShapeDtypeStruct((n_slots * 4, q_rows, width), BF16),
            jax.ShapeDtypeStruct((n_slots, q_rows, width), BF16),
        ],
        name="norm_in_rows",
    )(places, blocks, gain_row)


def whole_rows(parts, places, n_slots):
    _, q_rows, width = parts[0].shape

    def kernel(places_ref, *refs):
        out_ref = refs[4]
        for k in range(4):
            at = pl.multiple_of(places_ref[1 + k] * q_rows, q_rows)

            @pl.when(places_ref[0] == 0)
            def _():
                out_ref[0, pl.ds(at, q_rows), :] = refs[k][0]

            @pl.when(places_ref[0] != 0)
            def _():
                out_ref[0, pl.ds(at, q_rows), :] = cols_swapped(refs[k][0])

    return pl.pallas_call(
        kernel,
        grid_spec=pltpu.PrefetchScalarGridSpec(
            num_scalar_prefetch=1,
            grid=(n_slots,),
            in_specs=[pl.BlockSpec((1, q_rows, width), lambda i, p: (i, 0, 0))] * 4,
            out_specs=pl.BlockSpec((1, 4 * q_rows, width), lambda i, p: (i, 0, 0)),
        ),
        out_shape=jax.ShapeDtypeStruct((n_slots, 4 * q_rows, width), BF16),
        name="whole_rows",
    )(places, *parts)


class Links:
    def __init__(self):
        self.n_shard = lax.axis_size("shard")
        self.shard = lax.axis_index("shard")
        self.z = lax.axis_index("ctx")
        self.t = lax.axis_index("tp")
        self.core = lax.rem(self.t, 2)
        self.y = self.t // 2
        c, y = self.core, self.y
        self.quarters = [2 * c + y, 2 * c + 1 - y, 2 * (1 - c) + y, 2 * (1 - c) + 1 - y]

    def swap_core(self, v):
        return lax.ppermute(v, "tp", CORE_SWAP)

    def swap_y(self, v):
        return lax.ppermute(v, "tp", Y_SWAP)

    def swap_shard(self, v):
        return lax.ppermute(v, "shard", SHARD_SWAP)

    def reduce_quarters(self, p):
        q = p.shape[0] // 4
        p = p.astype(BF16)
        r = self.swap_core(p[2 * q :])
        other = (p[q : 2 * q].astype(F32) + r[q:].astype(F32)).astype(BF16)
        r2 = self.swap_y(other)
        return p[:q].astype(F32) + r[:q].astype(F32) + r2.astype(F32)

    def quarters_of(self, v):
        y = self.swap_y(v)
        c = self.swap_core(v)
        yc = self.swap_core(y)
        return [v, y, c, yc]

    def gather_quarters(self, v):
        return jnp.concatenate(self.quarters_of(v))

    def gather_shard(self, v, axis):
        if self.n_shard != 2:
            return lax.all_gather(v, "shard", axis=axis, tiled=True)
        return jnp.concatenate([v, self.swap_shard(v)], axis)


def body(
    hidden_in,
    cotangent,
    lengths,
    positions,
    w_query,
    w_key,
    w_value,
    w_out,
    w_gate,
    w_up,
    w_down,
    g_input,
    g_post_attn,
    g_pre_ffn,
    g_post_ffn,
    q_gain,
    k_gain,
):
    ln = Links()
    n, slot_rows, width = hidden_in.shape
    q_rows = slot_rows // 4
    part = n * q_rows
    two = ln.n_shard == 2
    wide = width // ln.n_shard
    scale = HEAD_DIM ** (-0.5)
    slots = range(n)

    swapped = (ln.shard == 1).astype(jnp.int32) if two else jnp.int32(0)
    places = jnp.stack(
        [swapped] + [s * 4 + ln.quarters[k] for k in range(4) for s in slots]
    ).astype(jnp.int32)
    row_places = jnp.stack([swapped] + ln.quarters).astype(jnp.int32)

    gain_in = ln.gather_shard(g_input, 0).astype(F32)
    if two:
        mix = jnp.concatenate([w_query, pick(ln.core == 0, w_key, w_value)], 1)
        mix = ln.swap_shard(mix)
        query_w = jnp.concatenate([w_query, mix[:, :HEAD_DIM]], 0)
        r = mix[:, HEAD_DIM:]
        r_c = ln.swap_core(r)
        kv_w = jnp.concatenate(
            [
                jnp.concatenate([w_key, w_value], 1),
                jnp.concatenate([pick(ln.core == 0, r, r_c), pick(ln.core == 0, r_c, r)], 1),
            ],
            0,
        )
    else:
        query_w = ln.gather_shard(w_query, 0)
        kv_w = ln.gather_shard(jnp.concatenate([w_key, w_value], 1), 0)
    packed = jnp.concatenate([g_post_attn, g_pre_ffn, g_post_ffn, q_gain, k_gain])
    if two:
        gains = jnp.stack([packed, ln.swap_shard(packed)]).astype(F32)
    else:
        gains = lax.all_gather(packed, "shard").astype(F32)
    cuts = [0]
    for g in (g_post_attn, g_pre_ffn, g_post_ffn, q_gain, k_gain):
        cuts.append(cuts[-1] + g.shape[0])
    gain_attn, gain_ffn_in, gain_ffn_out, gain_query, gain_key = [
        gains[:, cuts[i] : cuts[i + 1]].reshape(-1) for i in range(5)
    ]
    if two:
        swap_head = lambda g: pick(swapped == 1, cols_swapped(g), g)
        gain_query, gain_key = swap_head(gain_query), swap_head(gain_key)
    out_w = ln.gather_shard(w_out, 1)

    odd = lax.rem(ln.z, 2) == 1

    def fetch_x(w):
        half = w.shape[0] // 2
        w = after(mix, w)
        return ln.swap_shard(lax.dynamic_slice_in_dim(w, pick(odd, half, 0), half, 0))

    def fetch_z(r):
        return lax.ppermute(r, "ctx", Z_PAIRS)

    def complete(w, r, r2, axis):
        other = jnp.concatenate([pick(odd, r2, r), pick(odd, r, r2)], 0)
        return jnp.concatenate([w, other], axis)

    frequency = jnp.exp(
        jnp.arange(HEAD_DIM // 2, dtype=F32) * (-2.0 * math.log(1000000.0) / HEAD_DIM)
    )
    key_order = jnp.stack(
        [lax.rem(ln.z - d + 4, 4) * 4 + ln.quarters[k] for k in range(4) for d in range(4)]
    )
    key_at = jnp.take(positions.reshape(n, 16, q_rows), key_order, axis=1)
    rows_at = key_at.reshape(n, 4, 4, q_rows)[:, :, 0].reshape(n, slot_rows)
    key_at = key_at.reshape(n, 16 * q_rows)
    angle = rows_at.astype(F32)[:, :, None] * frequency
    cosine, sine = jnp.cos(angle), jnp.sin(angle)
    cosine_k, sine_k = cosine[:, :q_rows], sine[:, :q_rows]

    normed, hid = norm_in_rows(hidden_in, gain_in[None], places)
    normed = normed.reshape(4 * part, width)
    hid = hid.reshape(part, width)

    kv_raw = mm(normed[:part], kv_w).reshape(n, q_rows, 2 * HEAD_DIM)
    k_raw, v_raw = kv_raw[..., :HEAD_DIM], kv_raw[..., HEAD_DIM:]
    k_rot = rope(norm_rows(k_raw, gain_key), cosine_k, sine_k).astype(BF16)
    kv_own = jnp.concatenate([k_rot, v_raw.astype(BF16)], -1)
    kv_far = [
        lax.ppermute(kv_own, "ctx", [(i, (i + d) % 4) for i in range(4)]) for d in (1, 2, 3)
    ]
    kv_near_y = ln.swap_y(kv_own)
    queries = mm(normed, query_w)
    if two:
        x_gate = fetch_x(w_gate)
        x_gate, kv_far, kv_near_y, queries = lax.optimization_barrier(
            (x_gate, kv_far, kv_near_y, queries)
        )
    kv_far = jnp.stack(kv_far, 1)
    kv_far_y = ln.swap_y(kv_far)
    if two:
        x_up = fetch_x(w_up)
        z_gate = fetch_z(x_gate)
        x_up, z_gate, kv_far_y = lax.optimization_barrier((x_up, z_gate, kv_far_y))
    kv_both = jnp.concatenate([kv_own[:, None], kv_far, kv_near_y[:, None], kv_far_y], 1)
    kv_whole = jnp.concatenate([kv_both, ln.swap_core(kv_both)], 1)
    kv_whole = kv_whole.reshape(n, 16 * q_rows, 2 * HEAD_DIM)
    key_all = [kv_whole[s, :, :HEAD_DIM] for s in slots]
    value_all = [kv_whole[s, :, HEAD_DIM:] for s in slots]

    def by_slot(v):
        return v.reshape(4, n, q_rows, -1).swapaxes(0, 1).reshape(n, slot_rows, -1)

    def by_quarter(v):
        return v.reshape(n, 4, q_rows, -1).swapaxes(0, 1).reshape(4 * part, -1)

    queries = by_slot(queries)
    query_rot = rope(norm_rows(queries, gain_query), cosine, sine).astype(BF16)

    def scores_of(s):
        allowed = (key_at[s][None, :] <= rows_at[s][:, None]) & (key_at[s] < lengths[s])[None, :]
        return jnp.where(allowed, against(query_rot[s], key_all[s]) * scale, NEG_LARGE)

    log_total, attn = [], []
    for s in slots:
        scores = scores_of(s)
        row_max = jnp.max(scores, axis=-1, keepdims=True)
        expo = jnp.exp(scores - row_max)
        totals = jnp.sum(expo, axis=-1, keepdims=True)
        log_total.append(row_max + jnp.log(totals))
        attn.append((mm(expo.astype(BF16), value_all[s]) / totals).astype(BF16))
    attn_low = by_quarter(jnp.stack(attn))
    projected = ln.reduce_quarters(mm(attn_low, out_w))
    if two:
        gate_w = complete(w_gate, x_gate, z_gate, 0)
    else:
        gate_w = ln.gather_shard(w_gate, 0)
        up_w = ln.gather_shard(w_up, 0)
        down_w = ln.gather_shard(w_down, 1)

    x1 = hid.astype(F32) + norm_rows(projected, gain_attn)
    f_own = norm_rows(x1, gain_ffn_in).astype(BF16)
    if two:
        z_up = fetch_z(x_up)
        x_down = fetch_x(w_down)
        f_y = ln.swap_y(f_own)
        z_up, x_down, f_y = lax.optimization_barrier((z_up, x_down, f_y))
        up_w = complete(w_up, x_up, z_up, 0)
        ffn_low = jnp.concatenate([f_own, f_y, ln.swap_core(f_own), ln.swap_core(f_y)])
    else:
        ffn_low = ln.gather_quarters(f_own)

    gate = mm(ffn_low, gate_w)
    up = mm(ffn_low, up_w)
    k0 = math.sqrt(2.0 / math.pi)
    th = jnp.tanh(k0 * (gate + 0.044715 * gate * gate * gate))
    gel = 0.5 * gate * (1.0 + th)
    slope = 0.5 * (1.0 + th) + 0.5 * gate * (1.0 - th * th) * k0 * (1.0 + 3 * 0.044715 * gate * gate)
    middle = (gel * up).astype(BF16)
    to_up = gel.astype(BF16)
    to_gate = (up * slope).astype(BF16)
    if two:
        z_down = fetch_z(x_down)
        middle, to_up, to_gate, z_down = lax.optimization_barrier((middle, to_up, to_gate, z_down))
        down_w = complete(w_down, x_down, z_down, 1)
    down = ln.reduce_quarters(mm(middle, down_w))

    out_own = (x1 + norm_rows(down, gain_ffn_out)).astype(BF16)
    cot = lax.dynamic_slice_in_dim(cotangent, ln.quarters[0] * q_rows, q_rows, 1).reshape(part, width)
    if two:
        cot = pick(swapped == 1, cols_swapped(cot), cot)
    live = (rows_at[:, :q_rows] < lengths[:, None]).astype(F32).reshape(part, 1)
    gy = cot.astype(F32) * live
    dd = norm_back(down, gain_ffn_out, gy)
    d_down = ln.gather_quarters(dd.astype(BF16))

    inner = (ln.z == 1) | (ln.z == 2)

    alive = []

    def added(u, v):
        return (u.astype(F32) + v.astype(F32)).astype(BF16)

    class Piece:
        def __init__(self, own, oth, stage):
            self.v, self.r, self.stage = own, oth, stage
            alive.append(self)

        def over_shard(self, hold):
            self.v, self.r = added(hold(self.v), ln.swap_shard(self.r)), self.r[:0]

        def middle_hop(self):
            self.r = lax.ppermute(self.v, "ctx", [(1, 2), (2, 1)])

    def outer_hops(inward, outward, hold):
        if outward is None:
            inward.v = added(hold(inward.v), lax.ppermute(inward.v, "ctx", [(0, 1), (3, 2)]))
            return
        total = added(outward.v, outward.r)
        if inward is None:
            r = lax.ppermute(total, "ctx", [(1, 0), (2, 3)])
        else:
            r = lax.ppermute(pick(inner, total, inward.v), "ctx", Z_PAIRS)
            inward.v = added(hold(inward.v), r)
        outward.v, outward.r = pick(inner, hold(total), r), outward.r[:0]

    def pieces_of(v, count):
        v = row_major(v)
        if not two:
            v = lax.psum_scatter(v, "shard", scatter_dimension=0, tiled=True)
        step = wide // count
        return [
            Piece(
                v[i * step : (i + 1) * step],
                v[wide + i * step : wide + (i + 1) * step] if two else v[:0],
                0 if two else 1,
            )
            for i in range(count)
        ]

    def ready(*pieces):
        return [p for p in pieces if p.stage < 4]

    def tick(pieces, *values, first=()):
        hold = (lambda v: after(first, v)) if first else (lambda v: v)
        pieces = ready(*pieces)
        inward = [p for p in pieces if p.stage == 1]
        outward = [p for p in pieces if p.stage == 3]
        for p in inward:
            same = [q for q in outward if q.v.shape == p.v.shape][:1]
            outer_hops(p, same[0] if same else None, hold)
            outward = [q for q in outward if q not in same]
        for q in outward:
            outer_hops(None, q, hold)
        for p in pieces:
            if p.stage == 0:
                p.over_shard(hold)
            elif p.stage == 2:
                p.middle_hop()
            p.stage += 1
        state, values = lax.optimization_barrier(([(p.v, p.r) for p in alive], values))
        for p, (v, r) in zip(alive, state):
            p.v, p.r = v, r
        alive[:] = ready(*alive)
        return values[0] if len(values) == 1 else values

    grad_down_part = row_major(over_rows(d_down, middle).astype(BF16))
    grad_down_part, d_down_late = tick([], grad_down_part, d_down)
    d0, d1 = pieces_of(grad_down_part, 2)

    d_mid = against(d_down_late, down_w)
    d_gate = (d_mid * to_gate.astype(F32)).astype(BF16)
    d_up = (d_mid * to_up.astype(F32)).astype(BF16)
    d_part = against(d_gate, gate_w)
    d_gate, d_up, d_part = tick([d0], d_gate, d_up, d_part)
    d_part = (d_part + against(d_up, up_w)).astype(BF16)
    d_part_core = ln.swap_core(d_part[2 * part :])
    grad_gate_part = row_major(over_rows(ffn_low, after(d_part, d_gate)).astype(BF16))
    d_up, d_part, d_part_core, grad_gate_part = tick(
        [d0, d1], d_up, d_part, d_part_core, grad_gate_part
    )
    g0, g1 = pieces_of(grad_gate_part, 2)

    d_part_y = ln.swap_y(added(d_part[part : 2 * part], d_part_core[part:]))
    grad_up_part = row_major(over_rows(ffn_low, d_up).astype(BF16))
    d_part_y, grad_up_part = lax.optimization_barrier((d_part_y, grad_up_part))
    d_ffn_in = (
        d_part[:part].astype(F32) + d_part_core[:part].astype(F32) + d_part_y.astype(F32)
    )
    back = norm_back(x1, gain_ffn_in, d_ffn_in)
    d_x1 = gy + back
    dp = norm_back(projected, gain_attn, d_x1).astype(BF16)
    dp_y = ln.swap_y(dp)
    grad_up_part, dp, d_x1 = tick([d0, d1, g0], grad_up_part, dp, d_x1)
    u0, u1 = pieces_of(grad_up_part, 2)

    dp_both = jnp.concatenate([dp, dp_y])
    d_proj = jnp.concatenate([dp_both, ln.swap_core(dp_both)])
    out_y = ln.swap_y(after(dp_y, out_own))
    d_attn = by_slot(against(d_proj, out_w).astype(BF16))

    def attn_back(s):
        probs = jnp.exp(scores_of(s) - log_total[s])
        d_probs = against(d_attn[s], value_all[s])
        row_dot = jnp.sum(probs * d_probs, axis=-1, keepdims=True)
        d_scores = (probs * (d_probs - row_dot)).astype(BF16)
        d_query_rot = mm(d_scores, key_all[s]) * scale
        d_key_rot = (over_rows(d_scores, query_rot[s]) * scale).astype(BF16)
        d_value = over_rows(probs.astype(BF16), d_attn[s]).astype(BF16)
        return d_query_rot, jnp.concatenate([d_key_rot, d_value], 1)

    d_query_rot, d_kv = [], []
    for s in slots:
        dq_s, dkv_s = attn_back(s)
        h = dkv_s.shape[0] // 2
        d_query_rot.append(dq_s)
        d_kv.append(added(dkv_s[:h], ln.swap_core(dkv_s[h:])))
    d_kv = jnp.stack(d_kv)
    d_query_rot, d_kv, d_proj, out_y, out_own = tick(
        [d0, d1, g0, g1], d_query_rot, d_kv, d_proj, out_y, out_own, first=d_query_rot
    )

    h = d_kv.shape[1] // 2
    d_kv = added(d_kv[:, :h], ln.swap_y(d_kv[:, h:])).reshape(n, 4, q_rows, 2 * HEAD_DIM)
    out_c = ln.swap_core(out_own)
    d_query_turned = rope_back(jnp.stack(d_query_rot), cosine, sine)
    d_query = by_quarter(norm_back(queries, gain_query, d_query_turned).astype(BF16))
    saved = after(d_proj, x1, d_ffn_in, projected, d_x1, down, gy)
    dg_ffn_in, dg_attn, dg_ffn_out = [gain_back(*saved[i : i + 2]) for i in (0, 2, 4)]
    d_kv, d_query, d_query_turned, out_c, dg_ffn_in, dg_attn, dg_ffn_out = tick(
        [d1, g0, g1, u0], d_kv, d_query, d_query_turned, out_c, dg_ffn_in, dg_attn, dg_ffn_out
    )

    far = [
        lax.ppermute(d_kv[:, d], "ctx", [(i, (i - d) % 4) for i in range(4)]) for d in (1, 2, 3)
    ]
    d_in_part = against(d_query, query_w).astype(BF16)
    d_in_core = ln.swap_core(d_in_part[2 * part :])
    grad_oq = jnp.concatenate(
        [over_rows(d_proj, attn_low).astype(BF16), over_rows(normed, d_query).astype(BF16)], 1
    )
    dg_query = gain_back(queries, d_query_turned)
    far, d_kv, d_in_part, d_in_core, grad_oq, dg_query = tick(
        [u1] if two else [], far, d_kv, d_in_part, d_in_core, grad_oq, dg_query
    )
    (oq,) = pieces_of(grad_oq, 1)

    d_in_near = added(d_in_part[part : 2 * part], d_in_core[part:])
    d_kv_sum = (
        d_kv[:, 0].astype(F32) + far[0].astype(F32) + far[1].astype(F32) + far[2].astype(F32)
    )
    d_in_y = ln.swap_y(after(d_kv_sum, d_in_near))
    d_key_turned = rope_back(d_kv_sum[..., :HEAD_DIM], cosine_k, sine_k)
    dk, dg_key = norm_back(k_raw, gain_key, d_key_turned), gain_back(k_raw, d_key_turned)
    d_kv = jnp.concatenate([dk, d_kv_sum[..., HEAD_DIM:]], -1).astype(BF16)
    d_kv = d_kv.reshape(part, 2 * HEAD_DIM)
    grad_kv = over_rows(normed[:part], d_kv).astype(BF16)
    g_k, g_v = grad_kv[:, :HEAD_DIM], grad_kv[:, HEAD_DIM:]
    kv = pick(ln.core == 0, g_k, g_v).astype(F32) + ln.swap_core(
        pick(ln.core == 0, g_v, g_k)
    ).astype(F32)
    d_in_own = against(d_kv, kv_w)
    dg_in = (
        jnp.sum(d_in_part.astype(F32) * normed.astype(F32), axis=0)
        + jnp.sum(d_in_own * normed[:part].astype(F32), axis=0)
    ) / (1.0 + gain_in)
    if two:
        dg_query, dg_key = swap_head(dg_query), swap_head(dg_key)
    vec = jnp.concatenate(
        [v.reshape(ln.n_shard, -1) for v in (dg_in, dg_attn, dg_ffn_in, dg_ffn_out, dg_query, dg_key)],
        1,
    )
    n_vec = vec.shape[1]
    vec = vec + ln.swap_core(vec)
    tail = jnp.pad(vec, ((0, 0), (0, 16 * HEAD_DIM - n_vec))).reshape(ln.n_shard, 16, HEAD_DIM)
    tail = jnp.concatenate([kv.reshape(ln.n_shard, wide, HEAD_DIM), tail], 1).astype(BF16)
    if two:
        tail = added(tail[0], ln.swap_shard(tail[1]))
    else:
        tail = tail.reshape(ln.n_shard * (wide + 16), HEAD_DIM)
        tail = lax.psum_scatter(tail, "shard", scatter_dimension=0, tiled=True)
    tail, d_in_y, d_in_own = tick([g0, g1, u0, oq], tail, d_in_y, d_in_own)

    tail = added(tail, ln.swap_y(tail))
    d_in = (
        d_in_part[:part].astype(F32)
        + d_in_core[:part].astype(F32)
        + d_in_y.astype(F32)
        + d_in_own
    )
    grad_x_own = (d_x1 + norm_back(hid.astype(F32), gain_in, d_in)).astype(BF16)
    grad_down = jnp.concatenate([d0.v, d1.v]).T.astype(F32)
    tail, grad_x_own, grad_down = tick([g1, u0, u1], tail, grad_x_own, grad_down)
    last = Piece(tail, tail[:0], 1)

    gx_y = ln.swap_y(grad_x_own)
    gx_y = tick([last, u0, u1, oq], gx_y)
    gx_c, gx_yc, out_yc = ln.swap_core(grad_x_own), ln.swap_core(gx_y), ln.swap_core(out_y)
    grad_gate = jnp.concatenate([g0.v, g1.v]).astype(F32)
    gx_c, gx_yc, out_yc, grad_gate = tick([last, oq, u1], gx_c, gx_yc, out_yc, grad_gate)
    while ready(last, oq, d0, d1, g0, g1, u0, u1):
        tick([last, oq, d0, d1, g0, g1, u0, u1])

    grad_up = jnp.concatenate([u0.v, u1.v]).astype(F32)
    small = oq.v.astype(F32)
    grad_wo = small[:, :HEAD_DIM].T
    grad_wq = small[:, HEAD_DIM:]
    small = last.v
    vec = small[wide:].reshape(-1)[:n_vec].astype(F32)
    kv = small[:wide]
    kv_c = ln.swap_core(kv)
    grad_wk = pick(ln.core == 0, kv, kv_c).astype(F32)
    grad_wv = pick(ln.core == 0, kv_c, kv).astype(F32)

    cuts = [0]
    for g in (g_input, g_post_attn, g_pre_ffn, g_post_ffn, q_gain, k_gain):
        cuts.append(cuts[-1] + g.shape[0])
    gain_grads = [vec[cuts[i] : cuts[i + 1]] for i in range(6)]

    def assembled(parts):
        return whole_rows([u.reshape(n, q_rows, width) for u in parts], row_places, n)

    return (
        assembled([out_own, out_y, out_c, out_yc]),
        assembled([grad_x_own, gx_y, gx_c, gx_yc]),
        grad_wq,
        grad_wk,
        grad_wv,
        grad_wo,
        grad_gate,
        grad_up,
        grad_down,
        *gain_grads,
    )


def solution(mesh):
    rows = P("shard", "ctx", None)
    vec = P("shard")
    cols = P("shard", "tp")
    down = P("tp", "shard")
    flat = P("shard", None)
    return jax.shard_map(
        body,
        mesh=mesh,
        in_specs=(rows, rows, vec, flat, cols, flat, flat, down, cols, cols, down)
        + (vec,) * 6,
        out_specs=(rows, rows, cols, flat, flat, down, cols, cols, down) + (vec,) * 6,
        check_vma=False,
    )
```

```python
import math

import jax
import jax.numpy as jnp
from jax import lax
from jax.experimental.layout import Layout, with_layout_constraint
from jax.experimental import pallas as pl
from jax.experimental.pallas import tpu as pltpu
from jax.sharding import PartitionSpec as P

HEAD_DIM = 256
NORM_EPS = 1e-06
NEG_LARGE = -1e30
F32 = jnp.float32
BF16 = jnp.bfloat16

CORE_SWAP = [(0, 1), (1, 0), (2, 3), (3, 2)]
Y_SWAP = [(0, 2), (2, 0), (1, 3), (3, 1)]
Z_PAIRS = [(0, 1), (1, 0), (2, 3), (3, 2)]
SHARD_SWAP = [(0, 1), (1, 0)]


def inv_rms(values_in):
    return lax.rsqrt(jnp.mean(values_in * values_in, axis=-1, keepdims=True) + NORM_EPS)


def norm_rows(values_in, gain_vec):
    return values_in * inv_rms(values_in) * (1.0 + gain_vec)


def norm_back(values_in, gain_vec, upstream):
    c = inv_rms(values_in)
    scaled = upstream * (1.0 + gain_vec)
    d_values = c * scaled - values_in * (c * c * c) * jnp.mean(
        values_in * scaled, axis=-1, keepdims=True
    )
    return d_values


def gain_back(values_in, upstream):
    rows = tuple(range(values_in.ndim - 1))
    return jnp.sum(upstream * values_in * inv_rms(values_in), axis=rows)


def rope(values_in, cosine, sine):
    half = values_in.shape[-1] // 2
    u1, u2 = values_in[..., :half], values_in[..., half:]
    return jnp.concatenate([u1 * cosine - u2 * sine, u2 * cosine + u1 * sine], axis=-1)


def rope_back(values_in, cosine, sine):
    half = values_in.shape[-1] // 2
    d1, d2 = values_in[..., :half], values_in[..., half:]
    return jnp.concatenate([d1 * cosine + d2 * sine, d2 * cosine - d1 * sine], axis=-1)


def mm(left, right):
    return jnp.dot(left, right, preferred_element_type=F32)


def over_rows(left, right):
    return lax.dot_general(left, right, (((0,), (0,)), ((), ())), preferred_element_type=F32)


def row_major(v):
    return with_layout_constraint(v, Layout(major_to_minor=tuple(range(v.ndim))))


def against(left, right):
    return lax.dot_general(left, right, (((1,), (1,)), ((), ())), preferred_element_type=F32)


def pick(flag, yes, no):
    return jnp.where(flag, yes, no)


def after(first, *values):
    kept = lax.optimization_barrier((first,) + values)[1:]
    return kept[0] if len(kept) == 1 else kept


def cols_swapped(v):
    half = v.shape[-1] // 2
    return jnp.concatenate([v[..., half:], v[..., :half]], axis=-1)


def norm_in_rows(hidden_in, gain_row, places):
    n_slots, slot_rows, width = hidden_in.shape
    q_rows = slot_rows // 4
    blocks = hidden_in.reshape(n_slots * 4, q_rows, width)

    def kernel(places_ref, h_ref, g_ref, normed_ref, own_ref):
        raw = h_ref[0]
        x = raw.astype(F32)
        c = lax.rsqrt(jnp.mean(x * x, axis=-1, keepdims=True) + NORM_EPS)
        first = pl.program_id(0) < n_slots

        def put(v):
            vf = v.astype(F32)
            normed_ref[0] = (vf * c * (1.0 + g_ref[...])).astype(BF16)

            @pl.when(first)
            def _():
                own_ref[0] = v

        @pl.when(places_ref[0] == 0)
        def _():
            put(raw)

        @pl.when(places_ref[0] != 0)
        def _():
            put(cols_swapped(raw))

    return pl.pallas_call(
        kernel,
        grid_spec=pltpu.PrefetchScalarGridSpec(
            num_scalar_prefetch=1,
            grid=(n_slots * 4,),
            in_specs=[
                pl.BlockSpec((1, q_rows, width), lambda i, p: (p[i + 1], 0, 0)),
                pl.BlockSpec((1, width), lambda i, p: (0, 0)),
            ],
            out_specs=[
                pl.BlockSpec((1, q_rows, width), lambda i, p: (i, 0, 0)),
                pl.BlockSpec(
                    (1, q_rows, width), lambda i, p: (jnp.minimum(i, n_slots - 1), 0, 0)
                ),
            ],
        ),
        out_shape=[
            jax.ShapeDtypeStruct((n_slots * 4, q_rows, width), BF16),
            jax.ShapeDtypeStruct((n_slots, q_rows, width), BF16),
        ],
        name="norm_in_rows",
    )(places, blocks, gain_row)


def whole_rows(parts, places, n_slots):
    _, q_rows, width = parts[0].shape

    def kernel(places_ref, *refs):
        out_ref = refs[4]
        for k in range(4):
            at = pl.multiple_of(places_ref[1 + k] * q_rows, q_rows)

            @pl.when(places_ref[0] == 0)
            def _():
                out_ref[0, pl.ds(at, q_rows), :] = refs[k][0]

            @pl.when(places_ref[0] != 0)
            def _():
                out_ref[0, pl.ds(at, q_rows), :] = cols_swapped(refs[k][0])

    return pl.pallas_call(
        kernel,
        grid_spec=pltpu.PrefetchScalarGridSpec(
            num_scalar_prefetch=1,
            grid=(n_slots,),
            in_specs=[pl.BlockSpec((1, q_rows, width), lambda i, p: (i, 0, 0))] * 4,
            out_specs=pl.BlockSpec((1, 4 * q_rows, width), lambda i, p: (i, 0, 0)),
        ),
        out_shape=jax.ShapeDtypeStruct((n_slots, 4 * q_rows, width), BF16),
        name="whole_rows",
    )(places, *parts)


class Links:
    def __init__(self):
        self.n_shard = lax.axis_size("shard")
        self.shard = lax.axis_index("shard")
        self.z = lax.axis_index("ctx")
        self.t = lax.axis_index("tp")
        self.core = lax.rem(self.t, 2)
        self.y = self.t // 2
        c, y = self.core, self.y
        self.quarters = [2 * c + y, 2 * c + 1 - y, 2 * (1 - c) + y, 2 * (1 - c) + 1 - y]

    def swap_core(self, v):
        return lax.ppermute(v, "tp", CORE_SWAP)

    def swap_y(self, v):
        return lax.ppermute(v, "tp", Y_SWAP)

    def swap_shard(self, v):
        return lax.ppermute(v, "shard", SHARD_SWAP)

    def reduce_quarters(self, p):
        q = p.shape[0] // 4
        p = p.astype(BF16)
        r = self.swap_core(p[2 * q :])
        other = (p[q : 2 * q].astype(F32) + r[q:].astype(F32)).astype(BF16)
        r2 = self.swap_y(other)
        return p[:q].astype(F32) + r[:q].astype(F32) + r2.astype(F32)

    def quarters_of(self, v):
        y = self.swap_y(v)
        c = self.swap_core(v)
        yc = self.swap_core(y)
        return [v, y, c, yc]

    def gather_quarters(self, v):
        return jnp.concatenate(self.quarters_of(v))

    def gather_shard(self, v, axis):
        if self.n_shard != 2:
            return lax.all_gather(v, "shard", axis=axis, tiled=True)
        return jnp.concatenate([v, self.swap_shard(v)], axis)


def body(
    hidden_in,
    cotangent,
    lengths,
    positions,
    w_query,
    w_key,
    w_value,
    w_out,
    w_gate,
    w_up,
    w_down,
    g_input,
    g_post_attn,
    g_pre_ffn,
    g_post_ffn,
    q_gain,
    k_gain,
):
    ln = Links()
    n, slot_rows, width = hidden_in.shape
    q_rows = slot_rows // 4
    part = n * q_rows
    two = ln.n_shard == 2
    wide = width // ln.n_shard
    scale = HEAD_DIM ** (-0.5)
    slots = range(n)

    swapped = (ln.shard == 1).astype(jnp.int32) if two else jnp.int32(0)
    places = jnp.stack(
        [swapped] + [s * 4 + ln.quarters[k] for k in range(4) for s in slots]
    ).astype(jnp.int32)
    row_places = jnp.stack([swapped] + ln.quarters).astype(jnp.int32)

    gain_in = ln.gather_shard(g_input, 0).astype(F32)
    if two:
        mix = jnp.concatenate([w_query, pick(ln.core == 0, w_key, w_value)], 1)
        mix = ln.swap_shard(mix)
        query_w = jnp.concatenate([w_query, mix[:, :HEAD_DIM]], 0)
        r = mix[:, HEAD_DIM:]
        r_c = ln.swap_core(r)
        kv_w = jnp.concatenate(
            [
                jnp.concatenate([w_key, w_value], 1),
                jnp.concatenate([pick(ln.core == 0, r, r_c), pick(ln.core == 0, r_c, r)], 1),
            ],
            0,
        )
    else:
        query_w = ln.gather_shard(w_query, 0)
        kv_w = ln.gather_shard(jnp.concatenate([w_key, w_value], 1), 0)
    packed = jnp.concatenate([g_post_attn, g_pre_ffn, g_post_ffn, q_gain, k_gain])
    if two:
        gains = jnp.stack([packed, ln.swap_shard(packed)]).astype(F32)
    else:
        gains = lax.all_gather(packed, "shard").astype(F32)
    cuts = [0]
    for g in (g_post_attn, g_pre_ffn, g_post_ffn, q_gain, k_gain):
        cuts.append(cuts[-1] + g.shape[0])
    gain_attn, gain_ffn_in, gain_ffn_out, gain_query, gain_key = [
        gains[:, cuts[i] : cuts[i + 1]].reshape(-1) for i in range(5)
    ]
    if two:
        swap_head = lambda g: pick(swapped == 1, cols_swapped(g), g)
        gain_query, gain_key = swap_head(gain_query), swap_head(gain_key)
    out_w = ln.gather_shard(w_out, 1)

    odd = lax.rem(ln.z, 2) == 1

    def fetch_x(w):
        half = w.shape[0] // 2
        w = after(mix, w)
        return ln.swap_shard(lax.dynamic_slice_in_dim(w, pick(odd, half, 0), half, 0))

    def fetch_z(r):
        return lax.ppermute(r, "ctx", Z_PAIRS)

    def complete(w, r, r2, axis):
        other = jnp.concatenate([pick(odd, r2, r), pick(odd, r, r2)], 0)
        return jnp.concatenate([w, other], axis)

    frequency = jnp.exp(
        jnp.arange(HEAD_DIM // 2, dtype=F32) * (-2.0 * math.log(1000000.0) / HEAD_DIM)
    )
    key_order = jnp.stack(
        [lax.rem(ln.z - d + 4, 4) * 4 + ln.quarters[k] for k in range(4) for d in range(4)]
    )
    key_at = jnp.take(positions.reshape(n, 16, q_rows), key_order, axis=1)
    rows_at = key_at.reshape(n, 4, 4, q_rows)[:, :, 0].reshape(n, slot_rows)
    key_at = key_at.reshape(n, 16 * q_rows)
    angle = rows_at.astype(F32)[:, :, None] * frequency
    cosine, sine = jnp.cos(angle), jnp.sin(angle)
    cosine_k, sine_k = cosine[:, :q_rows], sine[:, :q_rows]

    normed, hid = norm_in_rows(hidden_in, gain_in[None], places)
    normed = normed.reshape(4 * part, width)
    hid = hid.reshape(part, width)

    kv_raw = mm(normed[:part], kv_w).reshape(n, q_rows, 2 * HEAD_DIM)
    k_raw, v_raw = kv_raw[..., :HEAD_DIM], kv_raw[..., HEAD_DIM:]
    k_rot = rope(norm_rows(k_raw, gain_key), cosine_k, sine_k).astype(BF16)
    kv_own = jnp.concatenate([k_rot, v_raw.astype(BF16)], -1)
    kv_far = [
        lax.ppermute(kv_own, "ctx", [(i, (i + d) % 4) for i in range(4)]) for d in (1, 2, 3)
    ]
    kv_near_y = ln.swap_y(kv_own)
    queries = mm(normed, query_w)
    if two:
        x_gate = fetch_x(w_gate)
        x_gate, kv_far, kv_near_y, queries = lax.optimization_barrier(
            (x_gate, kv_far, kv_near_y, queries)
        )
    kv_far = jnp.stack(kv_far, 1)
    kv_far_y = ln.swap_y(kv_far)
    if two:
        x_up = fetch_x(w_up)
        z_gate = fetch_z(x_gate)
        x_up, z_gate, kv_far_y = lax.optimization_barrier((x_up, z_gate, kv_far_y))
    kv_both = jnp.concatenate([kv_own[:, None], kv_far, kv_near_y[:, None], kv_far_y], 1)
    kv_whole = jnp.concatenate([kv_both, ln.swap_core(kv_both)], 1)
    kv_whole = kv_whole.reshape(n, 16 * q_rows, 2 * HEAD_DIM)
    key_all = [kv_whole[s, :, :HEAD_DIM] for s in slots]
    value_all = [kv_whole[s, :, HEAD_DIM:] for s in slots]

    def by_slot(v):
        return v.reshape(4, n, q_rows, -1).swapaxes(0, 1).reshape(n, slot_rows, -1)

    def by_quarter(v):
        return v.reshape(n, 4, q_rows, -1).swapaxes(0, 1).reshape(4 * part, -1)

    queries = by_slot(queries)
    query_rot = rope(norm_rows(queries, gain_query), cosine, sine).astype(BF16)

    def scores_of(s):
        allowed = (key_at[s][None, :] <= rows_at[s][:, None]) & (key_at[s] < lengths[s])[None, :]
        return jnp.where(allowed, against(query_rot[s], key_all[s]) * scale, NEG_LARGE)

    log_total, attn = [], []
    for s in slots:
        scores = scores_of(s)
        row_max = jnp.max(scores, axis=-1, keepdims=True)
        expo = jnp.exp(scores - row_max)
        totals = jnp.sum(expo, axis=-1, keepdims=True)
        log_total.append(row_max + jnp.log(totals))
        attn.append((mm(expo.astype(BF16), value_all[s]) / totals).astype(BF16))
    attn_low = by_quarter(jnp.stack(attn))
    projected = ln.reduce_quarters(mm(attn_low, out_w))
    if two:
        gate_w = complete(w_gate, x_gate, z_gate, 0)
    else:
        gate_w = ln.gather_shard(w_gate, 0)
        up_w = ln.gather_shard(w_up, 0)
        down_w = ln.gather_shard(w_down, 1)

    x1 = hid.astype(F32) + norm_rows(projected, gain_attn)
    f_own = norm_rows(x1, gain_ffn_in).astype(BF16)
    if two:
        z_up = fetch_z(x_up)
        x_down = fetch_x(w_down)
        f_y = ln.swap_y(f_own)
        z_up, x_down, f_y = lax.optimization_barrier((z_up, x_down, f_y))
        up_w = complete(w_up, x_up, z_up, 0)
        ffn_low = jnp.concatenate([f_own, f_y, ln.swap_core(f_own), ln.swap_core(f_y)])
    else:
        ffn_low = ln.gather_quarters(f_own)

    gate = mm(ffn_low, gate_w)
    up = mm(ffn_low, up_w)
    k0 = math.sqrt(2.0 / math.pi)
    th = jnp.tanh(k0 * (gate + 0.044715 * gate * gate * gate))
    gel = 0.5 * gate * (1.0 + th)
    slope = 0.5 * (1.0 + th) + 0.5 * gate * (1.0 - th * th) * k0 * (1.0 + 3 * 0.044715 * gate * gate)
    middle = (gel * up).astype(BF16)
    to_up = gel.astype(BF16)
    to_gate = (up * slope).astype(BF16)
    if two:
        z_down = fetch_z(x_down)
        middle, to_up, to_gate, z_down = lax.optimization_barrier((middle, to_up, to_gate, z_down))
        down_w = complete(w_down, x_down, z_down, 1)
    down = ln.reduce_quarters(mm(middle, down_w))

    out_own = (x1 + norm_rows(down, gain_ffn_out)).astype(BF16)
    cot = lax.dynamic_slice_in_dim(cotangent, ln.quarters[0] * q_rows, q_rows, 1).reshape(part, width)
    if two:
        cot = pick(swapped == 1, cols_swapped(cot), cot)
    live = (rows_at[:, :q_rows] < lengths[:, None]).astype(F32).reshape(part, 1)
    gy = cot.astype(F32) * live
    dd = norm_back(down, gain_ffn_out, gy)
    d_down = ln.gather_quarters(dd.astype(BF16))

    inner = (ln.z == 1) | (ln.z == 2)

    alive = []

    def added(u, v):
        return (u.astype(F32) + v.astype(F32)).astype(BF16)

    class Piece:
        def __init__(self, own, oth, stage):
            self.v, self.r, self.stage = own, oth, stage
            alive.append(self)

        def over_shard(self, hold):
            self.v, self.r = added(hold(self.v), ln.swap_shard(self.r)), self.r[:0]

        def middle_hop(self):
            self.r = lax.ppermute(self.v, "ctx", [(1, 2), (2, 1)])

        def result(self):
            return pick(inner, self.v, self.r)

    def outer_hops(inward, outward, hold):
        if outward is None:
            inward.v = added(hold(inward.v), lax.ppermute(inward.v, "ctx", [(0, 1), (3, 2)]))
            return
        total = added(outward.v, outward.r)
        if inward is None:
            r = lax.ppermute(total, "ctx", [(1, 0), (2, 3)])
        else:
            r = lax.ppermute(pick(inner, total, inward.v), "ctx", Z_PAIRS)
            inward.v = added(hold(inward.v), r)
        outward.v, outward.r = total, r

    def pieces_of(v, count):
        v = row_major(v)
        if not two:
            v = lax.psum_scatter(v, "shard", scatter_dimension=0, tiled=True)
        step = wide // count
        return [
            Piece(
                v[i * step : (i + 1) * step],
                v[wide + i * step : wide + (i + 1) * step] if two else v[:0],
                0 if two else 1,
            )
            for i in range(count)
        ]

    def ready(*pieces):
        return [p for p in pieces if p.stage < 4]

    def tick(pieces, *values, first=()):
        hold = (lambda v: after(first, v)) if first else (lambda v: v)
        pieces = ready(*pieces)
        inward = [p for p in pieces if p.stage == 1]
        outward = [p for p in pieces if p.stage == 3]
        for p in inward:
            same = [q for q in outward if q.v.shape == p.v.shape][:1]
            outer_hops(p, same[0] if same else None, hold)
            outward = [q for q in outward if q not in same]
        for q in outward:
            outer_hops(None, q, hold)
        for p in pieces:
            if p.stage == 0:
                p.over_shard(hold)
            elif p.stage == 2:
                p.middle_hop()
            p.stage += 1
        state, values = lax.optimization_barrier(([(p.v, p.r) for p in alive], values))
        for p, (v, r) in zip(alive, state):
            p.v, p.r = v, r
        alive[:] = ready(*alive)
        return values[0] if len(values) == 1 else values

    grad_down_part = row_major(over_rows(d_down, middle).astype(BF16))
    grad_down_part, d_down_late = tick([], grad_down_part, d_down)
    d0, d1 = pieces_of(grad_down_part, 2)

    d_mid = against(d_down_late, down_w)
    d_gate = (d_mid * to_gate.astype(F32)).astype(BF16)
    d_up = (d_mid * to_up.astype(F32)).astype(BF16)
    d_part = against(d_gate, gate_w)
    d_gate, d_up, d_part = tick([d0], d_gate, d_up, d_part)
    d_part = (d_part + against(d_up, up_w)).astype(BF16)
    d_part_core = ln.swap_core(d_part[2 * part :])
    grad_gate_part = row_major(over_rows(ffn_low, after(d_part, d_gate)).astype(BF16))
    d_up, d_part, d_part_core, grad_gate_part = tick(
        [d0, d1], d_up, d_part, d_part_core, grad_gate_part
    )
    g0, g1 = pieces_of(grad_gate_part, 2)

    d_part_y = ln.swap_y(added(d_part[part : 2 * part], d_part_core[part:]))
    grad_up_part = row_major(over_rows(ffn_low, d_up).astype(BF16))
    d_part_y, grad_up_part = lax.optimization_barrier((d_part_y, grad_up_part))
    d_ffn_in = (
        d_part[:part].astype(F32) + d_part_core[:part].astype(F32) + d_part_y.astype(F32)
    )
    back = norm_back(x1, gain_ffn_in, d_ffn_in)
    d_x1 = gy + back
    dp = norm_back(projected, gain_attn, d_x1).astype(BF16)
    dp_y = ln.swap_y(dp)
    grad_up_part, dp, d_x1 = tick([d0, d1, g0], grad_up_part, dp, d_x1)
    u0, u1 = pieces_of(grad_up_part, 2)

    dp_both = jnp.concatenate([dp, dp_y])
    d_proj = jnp.concatenate([dp_both, ln.swap_core(dp_both)])
    out_y = ln.swap_y(after(dp_y, out_own))
    d_attn = by_slot(against(d_proj, out_w).astype(BF16))

    def attn_back(s):
        probs = jnp.exp(scores_of(s) - log_total[s])
        d_probs = against(d_attn[s], value_all[s])
        row_dot = jnp.sum(probs * d_probs, axis=-1, keepdims=True)
        d_scores = (probs * (d_probs - row_dot)).astype(BF16)
        d_query_rot = mm(d_scores, key_all[s]) * scale
        d_key_rot = (over_rows(d_scores, query_rot[s]) * scale).astype(BF16)
        d_value = over_rows(probs.astype(BF16), d_attn[s]).astype(BF16)
        return d_query_rot, jnp.concatenate([d_key_rot, d_value], 1)

    d_query_rot, d_kv = [], []
    for s in slots:
        dq_s, dkv_s = attn_back(s)
        h = dkv_s.shape[0] // 2
        d_query_rot.append(dq_s)
        d_kv.append(added(dkv_s[:h], ln.swap_core(dkv_s[h:])))
    d_kv = jnp.stack(d_kv)
    d_query_rot, d_kv, d_proj, out_y, out_own = tick(
        [d0, d1, g0, g1], d_query_rot, d_kv, d_proj, out_y, out_own, first=d_query_rot
    )

    h = d_kv.shape[1] // 2
    d_kv = added(d_kv[:, :h], ln.swap_y(d_kv[:, h:])).reshape(n, 4, q_rows, 2 * HEAD_DIM)
    out_c = ln.swap_core(out_own)
    d_query_turned = rope_back(jnp.stack(d_query_rot), cosine, sine)
    d_query = by_quarter(norm_back(queries, gain_query, d_query_turned).astype(BF16))
    saved = after(d_proj, x1, d_ffn_in, projected, d_x1, down, gy)
    dg_ffn_in, dg_attn, dg_ffn_out = [gain_back(*saved[i : i + 2]) for i in (0, 2, 4)]
    d_kv, d_query, d_query_turned, out_c, dg_ffn_in, dg_attn, dg_ffn_out = tick(
        [d1, g0, g1, u0], d_kv, d_query, d_query_turned, out_c, dg_ffn_in, dg_attn, dg_ffn_out
    )

    far = [
        lax.ppermute(d_kv[:, d], "ctx", [(i, (i - d) % 4) for i in range(4)]) for d in (1, 2, 3)
    ]
    d_in_part = against(d_query, query_w).astype(BF16)
    d_in_core = ln.swap_core(d_in_part[2 * part :])
    grad_oq = jnp.concatenate(
        [over_rows(d_proj, attn_low).astype(BF16), over_rows(normed, d_query).astype(BF16)], 1
    )
    dg_query = gain_back(queries, d_query_turned)
    far, d_kv, d_in_part, d_in_core, grad_oq, dg_query = tick(
        [u1] if two else [], far, d_kv, d_in_part, d_in_core, grad_oq, dg_query
    )
    (oq,) = pieces_of(grad_oq, 1)

    d_in_near = added(d_in_part[part : 2 * part], d_in_core[part:])
    d_kv_sum = (
        d_kv[:, 0].astype(F32) + far[0].astype(F32) + far[1].astype(F32) + far[2].astype(F32)
    )
    d_in_y = ln.swap_y(after(d_kv_sum, d_in_near))
    d_key_turned = rope_back(d_kv_sum[..., :HEAD_DIM], cosine_k, sine_k)
    dk, dg_key = norm_back(k_raw, gain_key, d_key_turned), gain_back(k_raw, d_key_turned)
    d_kv = jnp.concatenate([dk, d_kv_sum[..., HEAD_DIM:]], -1).astype(BF16)
    d_kv = d_kv.reshape(part, 2 * HEAD_DIM)
    grad_kv = over_rows(normed[:part], d_kv).astype(BF16)
    g_k, g_v = grad_kv[:, :HEAD_DIM], grad_kv[:, HEAD_DIM:]
    kv = pick(ln.core == 0, g_k, g_v).astype(F32) + ln.swap_core(
        pick(ln.core == 0, g_v, g_k)
    ).astype(F32)
    d_in_own = against(d_kv, kv_w)
    dg_in = (
        jnp.sum(d_in_part.astype(F32) * normed.astype(F32), axis=0)
        + jnp.sum(d_in_own * normed[:part].astype(F32), axis=0)
    ) / (1.0 + gain_in)
    if two:
        dg_query, dg_key = swap_head(dg_query), swap_head(dg_key)
    vec = jnp.concatenate(
        [v.reshape(ln.n_shard, -1) for v in (dg_in, dg_attn, dg_ffn_in, dg_ffn_out, dg_query, dg_key)],
        1,
    )
    n_vec = vec.shape[1]
    vec = vec + ln.swap_core(vec)
    tail = jnp.pad(vec, ((0, 0), (0, 16 * HEAD_DIM - n_vec))).reshape(ln.n_shard, 16, HEAD_DIM)
    tail = jnp.concatenate([kv.reshape(ln.n_shard, wide, HEAD_DIM), tail], 1).astype(BF16)
    if two:
        tail = added(tail[0], ln.swap_shard(tail[1]))
    else:
        tail = tail.reshape(ln.n_shard * (wide + 16), HEAD_DIM)
        tail = lax.psum_scatter(tail, "shard", scatter_dimension=0, tiled=True)
    tail, d_in_own = tick([g0, g1, u0, oq], tail, d_in_own)

    tail = added(tail, ln.swap_y(tail))
    d_in = (
        d_in_part[:part].astype(F32)
        + d_in_core[:part].astype(F32)
        + d_in_y.astype(F32)
        + d_in_own
    )
    grad_x_own = (d_x1 + norm_back(hid.astype(F32), gain_in, d_in)).astype(BF16)
    grad_down = jnp.concatenate([d0.result(), d1.result()]).T.astype(F32)
    tail, grad_x_own, grad_down = tick([g1, u0, u1], tail, grad_x_own, grad_down)
    last = Piece(tail, tail[:0], 1)

    gx_y = ln.swap_y(grad_x_own)
    gx_y = tick([last, u0, u1, oq], gx_y)
    gx_c, gx_yc, out_yc = ln.swap_core(grad_x_own), ln.swap_core(gx_y), ln.swap_core(out_y)
    grad_gate = jnp.concatenate([g0.result(), g1.result()]).astype(F32)
    gx_c, gx_yc, out_yc, grad_gate = tick([last, oq, u1], gx_c, gx_yc, out_yc, grad_gate)
    while ready(last, oq, d0, d1, g0, g1, u0, u1):
        tick([last, oq, d0, d1, g0, g1, u0, u1])

    grad_up = jnp.concatenate([u0.result(), u1.result()]).astype(F32)
    small = oq.result().astype(F32)
    grad_wo = small[:, :HEAD_DIM].T
    grad_wq = small[:, HEAD_DIM:]
    small = last.result()
    vec = small[wide:].reshape(-1)[:n_vec].astype(F32)
    kv = small[:wide]
    kv_c = ln.swap_core(kv)
    grad_wk = pick(ln.core == 0, kv, kv_c).astype(F32)
    grad_wv = pick(ln.core == 0, kv_c, kv).astype(F32)

    cuts = [0]
    for g in (g_input, g_post_attn, g_pre_ffn, g_post_ffn, q_gain, k_gain):
        cuts.append(cuts[-1] + g.shape[0])
    gain_grads = [vec[cuts[i] : cuts[i + 1]] for i in range(6)]

    def assembled(parts):
        return whole_rows([u.reshape(n, q_rows, width) for u in parts], row_places, n)

    return (
        assembled([out_own, out_y, out_c, out_yc]),
        assembled([grad_x_own, gx_y, gx_c, gx_yc]),
        grad_wq,
        grad_wk,
        grad_wv,
        grad_wo,
        grad_gate,
        grad_up,
        grad_down,
        *gain_grads,
    )


def solution(mesh):
    rows = P("shard", "ctx", None)
    vec = P("shard")
    cols = P("shard", "tp")
    down = P("tp", "shard")
    flat = P("shard", None)
    return jax.shard_map(
        body,
        mesh=mesh,
        in_specs=(rows, rows, vec, flat, cols, flat, flat, down, cols, cols, down)
        + (vec,) * 6,
        out_specs=(rows, rows, cols, flat, flat, down, cols, cols, down) + (vec,) * 6,
        check_vma=False,
    )
```

```python
import math

import jax
import jax.numpy as jnp
from jax import lax
from jax.experimental.layout import Layout, with_layout_constraint
from jax.experimental import pallas as pl
from jax.experimental.pallas import tpu as pltpu
from jax.sharding import PartitionSpec as P

HEAD_DIM = 256
NORM_EPS = 1e-06
NEG_LARGE = -1e30
F32 = jnp.float32
BF16 = jnp.bfloat16

CORE_SWAP = [(0, 1), (1, 0), (2, 3), (3, 2)]
Y_SWAP = [(0, 2), (2, 0), (1, 3), (3, 1)]
Z_PAIRS = [(0, 1), (1, 0), (2, 3), (3, 2)]
SHARD_SWAP = [(0, 1), (1, 0)]


def inv_rms(values_in):
    return lax.rsqrt(jnp.mean(values_in * values_in, axis=-1, keepdims=True) + NORM_EPS)


def norm_rows(values_in, gain_vec):
    return values_in * inv_rms(values_in) * (1.0 + gain_vec)


def norm_back(values_in, gain_vec, upstream):
    c = inv_rms(values_in)
    scaled = upstream * (1.0 + gain_vec)
    d_values = c * scaled - values_in * (c * c * c) * jnp.mean(
        values_in * scaled, axis=-1, keepdims=True
    )
    return d_values


def gain_back(values_in, upstream):
    rows = tuple(range(values_in.ndim - 1))
    return jnp.sum(upstream * values_in * inv_rms(values_in), axis=rows)


def rope(values_in, cosine, sine):
    half = values_in.shape[-1] // 2
    u1, u2 = values_in[..., :half], values_in[..., half:]
    return jnp.concatenate([u1 * cosine - u2 * sine, u2 * cosine + u1 * sine], axis=-1)


def rope_back(values_in, cosine, sine):
    half = values_in.shape[-1] // 2
    d1, d2 = values_in[..., :half], values_in[..., half:]
    return jnp.concatenate([d1 * cosine + d2 * sine, d2 * cosine - d1 * sine], axis=-1)


def mm(left, right):
    return jnp.dot(left, right, preferred_element_type=F32)


def over_rows(left, right):
    return lax.dot_general(left, right, (((0,), (0,)), ((), ())), preferred_element_type=F32)


def row_major(v):
    return with_layout_constraint(v, Layout(major_to_minor=tuple(range(v.ndim))))


def against(left, right):
    return lax.dot_general(left, right, (((1,), (1,)), ((), ())), preferred_element_type=F32)


def pick(flag, yes, no):
    return jnp.where(flag, yes, no)


def after(first, *values):
    kept = lax.optimization_barrier((first,) + values)[1:]
    return kept[0] if len(kept) == 1 else kept


def cols_swapped(v):
    half = v.shape[-1] // 2
    return jnp.concatenate([v[..., half:], v[..., :half]], axis=-1)


def norm_in_rows(hidden_in, gain_row, places):
    n_slots, slot_rows, width = hidden_in.shape
    q_rows = slot_rows // 4
    blocks = hidden_in.reshape(n_slots, 4, q_rows, width)

    def kernel(places_ref, h_ref, g_ref, normed_ref, own_ref):
        def put(turned):
            for k in range(4):
                raw = h_ref[0, places_ref[1 + k]]
                x = raw.astype(F32)
                c = lax.rsqrt(jnp.mean(x * x, axis=-1, keepdims=True) + NORM_EPS)
                v = turned(raw)
                normed_ref[k, 0] = (v.astype(F32) * c * (1.0 + g_ref[...])).astype(BF16)
                if k == 0:
                    own_ref[0] = v

        @pl.when(places_ref[0] == 0)
        def _():
            put(lambda v: v)

        @pl.when(places_ref[0] != 0)
        def _():
            put(cols_swapped)

    return pl.pallas_call(
        kernel,
        grid_spec=pltpu.PrefetchScalarGridSpec(
            num_scalar_prefetch=1,
            grid=(n_slots,),
            in_specs=[
                pl.BlockSpec((1, 4, q_rows, width), lambda i, p: (i, 0, 0, 0)),
                pl.BlockSpec((1, width), lambda i, p: (0, 0)),
            ],
            out_specs=[
                pl.BlockSpec((4, 1, q_rows, width), lambda i, p: (0, i, 0, 0)),
                pl.BlockSpec((1, q_rows, width), lambda i, p: (i, 0, 0)),
            ],
        ),
        out_shape=[
            jax.ShapeDtypeStruct((4, n_slots, q_rows, width), BF16),
            jax.ShapeDtypeStruct((n_slots, q_rows, width), BF16),
        ],
        name="norm_in_rows",
    )(places, blocks, gain_row)


def whole_rows(parts, places, n_slots):
    _, q_rows, width = parts[0].shape

    def kernel(places_ref, *refs):
        out_ref = refs[4]
        for k in range(4):
            at = pl.multiple_of(places_ref[1 + k] * q_rows, q_rows)

            @pl.when(places_ref[0] == 0)
            def _():
                out_ref[0, pl.ds(at, q_rows), :] = refs[k][0]

            @pl.when(places_ref[0] != 0)
            def _():
                out_ref[0, pl.ds(at, q_rows), :] = cols_swapped(refs[k][0])

    return pl.pallas_call(
        kernel,
        grid_spec=pltpu.PrefetchScalarGridSpec(
            num_scalar_prefetch=1,
            grid=(n_slots,),
            in_specs=[pl.BlockSpec((1, q_rows, width), lambda i, p: (i, 0, 0))] * 4,
            out_specs=pl.BlockSpec((1, 4 * q_rows, width), lambda i, p: (i, 0, 0)),
        ),
        out_shape=jax.ShapeDtypeStruct((n_slots, 4 * q_rows, width), BF16),
        name="whole_rows",
    )(places, *parts)


class Links:
    def __init__(self):
        self.n_shard = lax.axis_size("shard")
        self.shard = lax.axis_index("shard")
        self.z = lax.axis_index("ctx")
        self.t = lax.axis_index("tp")
        self.core = lax.rem(self.t, 2)
        self.y = self.t // 2
        c, y = self.core, self.y
        self.quarters = [2 * c + y, 2 * c + 1 - y, 2 * (1 - c) + y, 2 * (1 - c) + 1 - y]

    def swap_core(self, v):
        return lax.ppermute(v, "tp", CORE_SWAP)

    def swap_y(self, v):
        return lax.ppermute(v, "tp", Y_SWAP)

    def swap_shard(self, v):
        return lax.ppermute(v, "shard", SHARD_SWAP)

    def reduce_quarters(self, p):
        q = p.shape[0] // 4
        p = p.astype(BF16)
        r = self.swap_core(p[2 * q :])
        other = (p[q : 2 * q].astype(F32) + r[q:].astype(F32)).astype(BF16)
        r2 = self.swap_y(other)
        return p[:q].astype(F32) + r[:q].astype(F32) + r2.astype(F32)

    def quarters_of(self, v):
        y = self.swap_y(v)
        c = self.swap_core(v)
        yc = self.swap_core(y)
        return [v, y, c, yc]

    def gather_quarters(self, v):
        return jnp.concatenate(self.quarters_of(v))

    def gather_shard(self, v, axis):
        if self.n_shard != 2:
            return lax.all_gather(v, "shard", axis=axis, tiled=True)
        return jnp.concatenate([v, self.swap_shard(v)], axis)


def body(
    hidden_in,
    cotangent,
    lengths,
    positions,
    w_query,
    w_key,
    w_value,
    w_out,
    w_gate,
    w_up,
    w_down,
    g_input,
    g_post_attn,
    g_pre_ffn,
    g_post_ffn,
    q_gain,
    k_gain,
):
    ln = Links()
    n, slot_rows, width = hidden_in.shape
    q_rows = slot_rows // 4
    part = n * q_rows
    two = ln.n_shard == 2
    wide = width // ln.n_shard
    scale = HEAD_DIM ** (-0.5)
    slots = range(n)

    swapped = (ln.shard == 1).astype(jnp.int32) if two else jnp.int32(0)
    row_places = jnp.stack([swapped] + ln.quarters).astype(jnp.int32)

    gain_in = ln.gather_shard(g_input, 0).astype(F32)
    if two:
        r = ln.swap_shard(pick(ln.core == 0, w_key, w_value))
        mix = ln.swap_shard(w_query)
        query_w = jnp.concatenate([w_query, mix], 0)
        r_c = ln.swap_core(r)
        kv_w = jnp.concatenate(
            [
                jnp.concatenate([w_key, w_value], 1),
                jnp.concatenate([pick(ln.core == 0, r, r_c), pick(ln.core == 0, r_c, r)], 1),
            ],
            0,
        )
    else:
        query_w = ln.gather_shard(w_query, 0)
        kv_w = ln.gather_shard(jnp.concatenate([w_key, w_value], 1), 0)
    packed = jnp.concatenate([g_post_attn, g_pre_ffn, g_post_ffn, q_gain, k_gain])
    if two:
        gains = jnp.stack([packed, ln.swap_shard(packed)]).astype(F32)
    else:
        gains = lax.all_gather(packed, "shard").astype(F32)
    cuts = [0]
    for g in (g_post_attn, g_pre_ffn, g_post_ffn, q_gain, k_gain):
        cuts.append(cuts[-1] + g.shape[0])
    gain_attn, gain_ffn_in, gain_ffn_out, gain_query, gain_key = [
        gains[:, cuts[i] : cuts[i + 1]].reshape(-1) for i in range(5)
    ]
    if two:
        swap_head = lambda g: pick(swapped == 1, cols_swapped(g), g)
        gain_query, gain_key = swap_head(gain_query), swap_head(gain_key)
    out_w = ln.gather_shard(w_out, 1)

    odd = lax.rem(ln.z, 2) == 1

    def fetch_x(w):
        half = w.shape[0] // 2
        w = after(mix, w)
        return ln.swap_shard(lax.dynamic_slice_in_dim(w, pick(odd, half, 0), half, 0))

    def fetch_z(r):
        return lax.ppermute(r, "ctx", Z_PAIRS)

    def complete(w, r, r2, axis):
        other = jnp.concatenate([pick(odd, r2, r), pick(odd, r, r2)], 0)
        return jnp.concatenate([w, other], axis)

    frequency = jnp.exp(
        jnp.arange(HEAD_DIM // 2, dtype=F32) * (-2.0 * math.log(1000000.0) / HEAD_DIM)
    )
    key_order = jnp.stack(
        [lax.rem(ln.z - d + 4, 4) * 4 + ln.quarters[k] for k in range(4) for d in range(4)]
    )
    key_at = jnp.take(positions.reshape(n, 16, q_rows), key_order, axis=1)
    rows_at = key_at.reshape(n, 4, 4, q_rows)[:, :, 0].reshape(n, slot_rows)
    key_at = key_at.reshape(n, 16 * q_rows)
    angle = rows_at.astype(F32)[:, :, None] * frequency
    cosine, sine = jnp.cos(angle), jnp.sin(angle)
    cosine_k, sine_k = cosine[:, :q_rows], sine[:, :q_rows]

    normed, hid = norm_in_rows(hidden_in, gain_in[None], row_places)
    normed = normed.reshape(4 * part, width)
    hid = hid.reshape(part, width)

    kv_raw = mm(normed[:part], kv_w).reshape(n, q_rows, 2 * HEAD_DIM)
    k_raw, v_raw = kv_raw[..., :HEAD_DIM], kv_raw[..., HEAD_DIM:]
    k_rot = rope(norm_rows(k_raw, gain_key), cosine_k, sine_k).astype(BF16)
    kv_own = jnp.concatenate([k_rot, v_raw.astype(BF16)], -1)
    kv_far = [
        lax.ppermute(kv_own, "ctx", [(i, (i + d) % 4) for i in range(4)]) for d in (1, 2, 3)
    ]
    kv_near_y = ln.swap_y(kv_own)
    queries = mm(normed, query_w)
    if two:
        x_gate = fetch_x(w_gate)
        x_gate, kv_far, kv_near_y, queries = lax.optimization_barrier(
            (x_gate, kv_far, kv_near_y, queries)
        )
    kv_far = jnp.stack(kv_far, 1)
    kv_far_y = ln.swap_y(kv_far)
    if two:
        x_up = fetch_x(w_up)
        z_gate = fetch_z(x_gate)
        x_up, z_gate, kv_far_y = lax.optimization_barrier((x_up, z_gate, kv_far_y))
    kv_both = jnp.concatenate([kv_own[:, None], kv_far, kv_near_y[:, None], kv_far_y], 1)
    kv_whole = jnp.concatenate([kv_both, ln.swap_core(kv_both)], 1)
    kv_whole = kv_whole.reshape(n, 16 * q_rows, 2 * HEAD_DIM)
    key_all = [kv_whole[s, :, :HEAD_DIM] for s in slots]
    value_all = [kv_whole[s, :, HEAD_DIM:] for s in slots]

    def by_slot(v):
        return v.reshape(4, n, q_rows, -1).swapaxes(0, 1).reshape(n, slot_rows, -1)

    def by_quarter(v):
        return v.reshape(n, 4, q_rows, -1).swapaxes(0, 1).reshape(4 * part, -1)

    queries = by_slot(queries)
    query_rot = rope(norm_rows(queries, gain_query), cosine, sine).astype(BF16)

    def scores_of(s):
        allowed = (key_at[s][None, :] <= rows_at[s][:, None]) & (key_at[s] < lengths[s])[None, :]
        return jnp.where(allowed, against(query_rot[s], key_all[s]) * scale, NEG_LARGE)

    log_total, attn = [], []
    for s in slots:
        scores = scores_of(s)
        row_max = jnp.max(scores, axis=-1, keepdims=True)
        expo = jnp.exp(scores - row_max)
        totals = jnp.sum(expo, axis=-1, keepdims=True)
        log_total.append(row_max + jnp.log(totals))
        attn.append((mm(expo.astype(BF16), value_all[s]) / totals).astype(BF16))
    attn_low = by_quarter(jnp.stack(attn))
    projected = ln.reduce_quarters(mm(attn_low, out_w))
    if two:
        gate_w = complete(w_gate, x_gate, z_gate, 0)
    else:
        gate_w = ln.gather_shard(w_gate, 0)
        up_w = ln.gather_shard(w_up, 0)
        down_w = ln.gather_shard(w_down, 1)

    x1 = hid.astype(F32) + norm_rows(projected, gain_attn)
    f_own = norm_rows(x1, gain_ffn_in).astype(BF16)
    if two:
        z_up = fetch_z(x_up)
        x_down = fetch_x(w_down)
        f_y = ln.swap_y(f_own)
        z_up, x_down, f_y = lax.optimization_barrier((z_up, x_down, f_y))
        up_w = complete(w_up, x_up, z_up, 0)
        ffn_low = jnp.concatenate([f_own, f_y, ln.swap_core(f_own), ln.swap_core(f_y)])
    else:
        ffn_low = ln.gather_quarters(f_own)

    gate = mm(ffn_low, gate_w)
    up = mm(ffn_low, up_w)
    k0 = math.sqrt(2.0 / math.pi)
    th = jnp.tanh(k0 * (gate + 0.044715 * gate * gate * gate))
    gel = 0.5 * gate * (1.0 + th)
    slope = 0.5 * (1.0 + th) + 0.5 * gate * (1.0 - th * th) * k0 * (1.0 + 3 * 0.044715 * gate * gate)
    middle = (gel * up).astype(BF16)
    to_up = gel.astype(BF16)
    to_gate = (up * slope).astype(BF16)
    if two:
        z_down = fetch_z(x_down)
        middle, to_up, to_gate, z_down = lax.optimization_barrier((middle, to_up, to_gate, z_down))
        down_w = complete(w_down, x_down, z_down, 1)
    down = ln.reduce_quarters(mm(middle, down_w))

    out_own = (x1 + norm_rows(down, gain_ffn_out)).astype(BF16)
    cot = lax.dynamic_slice_in_dim(cotangent, ln.quarters[0] * q_rows, q_rows, 1).reshape(part, width)
    if two:
        cot = pick(swapped == 1, cols_swapped(cot), cot)
    live = (rows_at[:, :q_rows] < lengths[:, None]).astype(F32).reshape(part, 1)
    gy = cot.astype(F32) * live
    dd = norm_back(down, gain_ffn_out, gy)
    d_down = ln.gather_quarters(dd.astype(BF16))

    inner = (ln.z == 1) | (ln.z == 2)

    alive = []

    def added(u, v):
        return (u.astype(F32) + v.astype(F32)).astype(BF16)

    class Piece:
        def __init__(self, own, oth, stage):
            self.v, self.r, self.stage = own, oth, stage
            alive.append(self)

        def over_shard(self, hold):
            self.v, self.r = added(hold(self.v), ln.swap_shard(self.r)), self.r[:0]

        def middle_hop(self):
            self.r = lax.ppermute(self.v, "ctx", [(1, 2), (2, 1)])

        def result(self):
            return pick(inner, self.v, self.r)

    def outer_hops(inward, outward, hold):
        if outward is None:
            inward.v = added(hold(inward.v), lax.ppermute(inward.v, "ctx", [(0, 1), (3, 2)]))
            return
        total = added(outward.v, outward.r)
        if inward is None:
            r = lax.ppermute(total, "ctx", [(1, 0), (2, 3)])
        else:
            r = lax.ppermute(pick(inner, total, inward.v), "ctx", Z_PAIRS)
            inward.v = added(hold(inward.v), r)
        outward.v, outward.r = total, r

    def pieces_of(v, count):
        v = row_major(v)
        if not two:
            v = lax.psum_scatter(v, "shard", scatter_dimension=0, tiled=True)
        step = wide // count
        return [
            Piece(
                v[i * step : (i + 1) * step],
                v[wide + i * step : wide + (i + 1) * step] if two else v[:0],
                0 if two else 1,
            )
            for i in range(count)
        ]

    def ready(*pieces):
        return [p for p in pieces if p.stage < 4]

    def tick(pieces, *values, first=()):
        hold = (lambda v: after(first, v)) if first else (lambda v: v)
        pieces = ready(*pieces)
        inward = [p for p in pieces if p.stage == 1]
        outward = [p for p in pieces if p.stage == 3]
        for p in inward:
            same = [q for q in outward if q.v.shape == p.v.shape][:1]
            outer_hops(p, same[0] if same else None, hold)
            outward = [q for q in outward if q not in same]
        for q in outward:
            outer_hops(None, q, hold)
        for p in pieces:
            if p.stage == 0:
                p.over_shard(hold)
            elif p.stage == 2:
                p.middle_hop()
            p.stage += 1
        state, values = lax.optimization_barrier(([(p.v, p.r) for p in alive], values))
        for p, (v, r) in zip(alive, state):
            p.v, p.r = v, r
        alive[:] = ready(*alive)
        return values[0] if len(values) == 1 else values

    grad_down_part = row_major(over_rows(d_down, middle).astype(BF16))
    grad_down_part, d_down_late = tick([], grad_down_part, d_down)
    d0, d1 = pieces_of(grad_down_part, 2)

    d_mid = against(d_down_late, down_w)
    d_gate = (d_mid * to_gate.astype(F32)).astype(BF16)
    d_up = (d_mid * to_up.astype(F32)).astype(BF16)
    d_part = against(d_gate, gate_w)
    d_gate, d_up, d_part = tick([d0], d_gate, d_up, d_part)
    d_part = (d_part + against(d_up, up_w)).astype(BF16)
    d_part_core = ln.swap_core(d_part[2 * part :])
    grad_gate_part = row_major(over_rows(ffn_low, after(d_part, d_gate)).astype(BF16))
    d_up, d_part, d_part_core, grad_gate_part = tick(
        [d0, d1], d_up, d_part, d_part_core, grad_gate_part
    )
    g0, g1 = pieces_of(grad_gate_part, 2)

    d_part_y = ln.swap_y(added(d_part[part : 2 * part], d_part_core[part:]))
    grad_up_part = row_major(over_rows(ffn_low, d_up).astype(BF16))
    d_part_y, grad_up_part = lax.optimization_barrier((d_part_y, grad_up_part))
    d_ffn_in = (
        d_part[:part].astype(F32) + d_part_core[:part].astype(F32) + d_part_y.astype(F32)
    )
    back = norm_back(x1, gain_ffn_in, d_ffn_in)
    d_x1 = gy + back
    dp = norm_back(projected, gain_attn, d_x1).astype(BF16)
    dp_y = ln.swap_y(dp)
    grad_up_part, dp, d_x1 = tick([d0, d1, g0], grad_up_part, dp, d_x1)
    u0, u1 = pieces_of(grad_up_part, 2)

    dp_both = jnp.concatenate([dp, dp_y])
    d_proj = jnp.concatenate([dp_both, ln.swap_core(dp_both)])
    out_y = ln.swap_y(after(dp_y, out_own))
    d_attn = by_slot(against(d_proj, out_w).astype(BF16))

    def attn_back(s):
        probs = jnp.exp(scores_of(s) - log_total[s])
        d_probs = against(d_attn[s], value_all[s])
        row_dot = jnp.sum(probs * d_probs, axis=-1, keepdims=True)
        d_scores = (probs * (d_probs - row_dot)).astype(BF16)
        d_query_rot = mm(d_scores, key_all[s]) * scale
        d_key_rot = (over_rows(d_scores, query_rot[s]) * scale).astype(BF16)
        d_value = over_rows(probs.astype(BF16), d_attn[s]).astype(BF16)
        return d_query_rot, jnp.concatenate([d_key_rot, d_value], 1)

    d_query_rot, d_kv = [], []
    for s in slots:
        dq_s, dkv_s = attn_back(s)
        h = dkv_s.shape[0] // 2
        d_query_rot.append(dq_s)
        d_kv.append(added(dkv_s[:h], ln.swap_core(dkv_s[h:])))
    d_kv = jnp.stack(d_kv)
    d_query_rot, d_kv, d_proj, out_y, out_own = tick(
        [d0, d1, g0, g1], d_query_rot, d_kv, d_proj, out_y, out_own, first=d_query_rot
    )

    h = d_kv.shape[1] // 2
    d_kv = added(d_kv[:, :h], ln.swap_y(d_kv[:, h:])).reshape(n, 4, q_rows, 2 * HEAD_DIM)
    out_c = ln.swap_core(out_own)
    d_query_turned = rope_back(jnp.stack(d_query_rot), cosine, sine)
    d_query = by_quarter(norm_back(queries, gain_query, d_query_turned).astype(BF16))
    saved = after(d_proj, x1, d_ffn_in, projected, d_x1, down, gy)
    dg_ffn_in, dg_attn, dg_ffn_out = [gain_back(*saved[i : i + 2]) for i in (0, 2, 4)]
    d_kv, d_query, d_query_turned, out_c, dg_ffn_in, dg_attn, dg_ffn_out = tick(
        [d1, g0, g1, u0], d_kv, d_query, d_query_turned, out_c, dg_ffn_in, dg_attn, dg_ffn_out
    )

    far = [
        lax.ppermute(d_kv[:, d], "ctx", [(i, (i - d) % 4) for i in range(4)]) for d in (1, 2, 3)
    ]
    d_in_part = against(d_query, query_w).astype(BF16)
    d_in_core = ln.swap_core(d_in_part[2 * part :])
    grad_oq = jnp.concatenate(
        [over_rows(d_proj, attn_low).astype(BF16), over_rows(normed, d_query).astype(BF16)], 1
    )
    dg_query = gain_back(queries, d_query_turned)
    far, d_kv, d_in_part, d_in_core, grad_oq, dg_query = tick(
        [u1] if two else [], far, d_kv, d_in_part, d_in_core, grad_oq, dg_query
    )
    (oq,) = pieces_of(grad_oq, 1)

    d_in_near = added(d_in_part[part : 2 * part], d_in_core[part:])
    d_kv_sum = (
        d_kv[:, 0].astype(F32) + far[0].astype(F32) + far[1].astype(F32) + far[2].astype(F32)
    )
    d_in_y = ln.swap_y(after(d_kv_sum, d_in_near))
    d_key_turned = rope_back(d_kv_sum[..., :HEAD_DIM], cosine_k, sine_k)
    dk, dg_key = norm_back(k_raw, gain_key, d_key_turned), gain_back(k_raw, d_key_turned)
    d_kv = jnp.concatenate([dk, d_kv_sum[..., HEAD_DIM:]], -1).astype(BF16)
    d_kv = d_kv.reshape(part, 2 * HEAD_DIM)
    grad_kv = over_rows(normed[:part], d_kv).astype(BF16)
    g_k, g_v = grad_kv[:, :HEAD_DIM], grad_kv[:, HEAD_DIM:]
    kv = pick(ln.core == 0, g_k, g_v).astype(F32) + ln.swap_core(
        pick(ln.core == 0, g_v, g_k)
    ).astype(F32)
    d_in_own = against(d_kv, kv_w)
    dg_in = (
        jnp.sum(d_in_part.astype(F32) * normed.astype(F32), axis=0)
        + jnp.sum(d_in_own * normed[:part].astype(F32), axis=0)
    ) / (1.0 + gain_in)
    if two:
        dg_query, dg_key = swap_head(dg_query), swap_head(dg_key)
    vec = jnp.concatenate(
        [v.reshape(ln.n_shard, -1) for v in (dg_in, dg_attn, dg_ffn_in, dg_ffn_out, dg_query, dg_key)],
        1,
    )
    n_vec = vec.shape[1]
    vec = vec + ln.swap_core(vec)
    tail = jnp.pad(vec, ((0, 0), (0, 16 * HEAD_DIM - n_vec))).reshape(ln.n_shard, 16, HEAD_DIM)
    tail = jnp.concatenate([kv.reshape(ln.n_shard, wide, HEAD_DIM), tail], 1).astype(BF16)
    if two:
        tail = added(tail[0], ln.swap_shard(tail[1]))
    else:
        tail = tail.reshape(ln.n_shard * (wide + 16), HEAD_DIM)
        tail = lax.psum_scatter(tail, "shard", scatter_dimension=0, tiled=True)
    tail, d_in_own = tick([g0, g1, u0, oq], tail, d_in_own)

    tail = added(tail, ln.swap_y(tail))
    d_in = (
        d_in_part[:part].astype(F32)
        + d_in_core[:part].astype(F32)
        + d_in_y.astype(F32)
        + d_in_own
    )
    grad_x_own = (d_x1 + norm_back(hid.astype(F32), gain_in, d_in)).astype(BF16)
    grad_down = jnp.concatenate([d0.result(), d1.result()]).T.astype(F32)
    tail, grad_x_own, grad_down = tick([g1, u0, u1], tail, grad_x_own, grad_down)
    last = Piece(tail, tail[:0], 1)

    gx_y = ln.swap_y(grad_x_own)
    gx_y = tick([last, u0, u1, oq], gx_y)
    gx_c, gx_yc, out_yc = ln.swap_core(grad_x_own), ln.swap_core(gx_y), ln.swap_core(out_y)
    grad_gate = jnp.concatenate([g0.result(), g1.result()]).astype(F32)
    gx_c, gx_yc, out_yc, grad_gate = tick([last, oq, u1], gx_c, gx_yc, out_yc, grad_gate)
    while ready(last, oq, d0, d1, g0, g1, u0, u1):
        tick([last, oq, d0, d1, g0, g1, u0, u1])

    grad_up = jnp.concatenate([u0.result(), u1.result()]).astype(F32)
    small = oq.result().astype(F32)
    grad_wo = small[:, :HEAD_DIM].T
    grad_wq = small[:, HEAD_DIM:]
    small = last.result()
    vec = small[wide:].reshape(-1)[:n_vec].astype(F32)
    kv = small[:wide]
    kv_c = ln.swap_core(kv)
    grad_wk = pick(ln.core == 0, kv, kv_c).astype(F32)
    grad_wv = pick(ln.core == 0, kv_c, kv).astype(F32)

    cuts = [0]
    for g in (g_input, g_post_attn, g_pre_ffn, g_post_ffn, q_gain, k_gain):
        cuts.append(cuts[-1] + g.shape[0])
    gain_grads = [vec[cuts[i] : cuts[i + 1]] for i in range(6)]

    def assembled(parts):
        return whole_rows([u.reshape(n, q_rows, width) for u in parts], row_places, n)

    return (
        assembled([out_own, out_y, out_c, out_yc]),
        assembled([grad_x_own, gx_y, gx_c, gx_yc]),
        grad_wq,
        grad_wk,
        grad_wv,
        grad_wo,
        grad_gate,
        grad_up,
        grad_down,
        *gain_grads,
    )


def solution(mesh):
    rows = P("shard", "ctx", None)
    vec = P("shard")
    cols = P("shard", "tp")
    down = P("tp", "shard")
    flat = P("shard", None)
    return jax.shard_map(
        body,
        mesh=mesh,
        in_specs=(rows, rows, vec, flat, cols, flat, flat, down, cols, cols, down)
        + (vec,) * 6,
        out_specs=(rows, rows, cols, flat, flat, down, cols, cols, down) + (vec,) * 6,
        check_vma=False,
    )
```
